512 devices in a mesh: dp: 16 (over z), mp: 32 (over y, x, core).
Axes of the slice: x: 4, y: 4, z: 16, core: 2. Of those that a mesh axis runs over, the one named last changes fastest.
Arguments:
- output_gradient: bfloat16 [12288, 8192], P('dp', 'mp'), may hold values from -6 to 6
- saved_gate_value: bfloat16 [12288, 14336], P('dp', 'mp'), may hold values from -6 to 6
- saved_up_value: bfloat16 [12288, 14336], P('dp', 'mp'), may hold values from -6 to 6
- down_weight: bfloat16 [14336, 8192], P('mp', 'dp'), may hold values from -0.046875 to 0.046875
- adapter_first_weight: bfloat16 [64, 64, 14336], P('dp', None, 'mp'), may hold values from -0.046875 to 0.046875
- adapter_second_weight: bfloat16 [64, 64, 8192], P('dp', None, 'mp'), may hold values from -0.0625 to 0.0625
- adapter_of_block: int32 [192], replicated, may hold values from 0 to 63, as said below
- slot_of_adapter: int32 [64], replicated, may hold values from 0 to 63, as said below
Outputs:
- d_gate: bfloat16 [12288, 14336], P('dp', 'mp')
- d_up: bfloat16 [12288, 14336], P('dp', 'mp')
- grad_a: float32 [64, 64, 14336], P('dp', None, 'mp')
- grad_b: float32 [64, 64, 8192], P('dp', None, 'mp')
The draws below stay inside these ranges and needn't reach their ends.
Inputs may be any that keep to these rules, and one draw needn't show every extreme that they name: `adapter_of_block`: block k holds tokens k * 64 to k * 64 + 63; group g holds blocks g * 12 onward. Slot s belongs to owner s // 4; the blocks of one group use adapters of any one owner at most 1 times, and in every draw one owner takes exactly 1 block of every group. A permutation: adapter a is stored at index slot_of_adapter[a] of adapter_first_weight, adapter_second_weight, grad_a and grad_b.
All inputs are finite; a program needn't handle non-finite values.
Results may differ from the reference program's by a relative error of at most 0.0057.
Values may be sent and summed in bfloat16 or wider, within the bound.
A program may use at most 128 MiB of HBM per device.

```python
import jax
import jax.numpy as jnp

MODEL_WIDTH = 8192
HIDDEN_UNITS = 14336
ADAPTER_RANK = 64
ADAPTER_TOTAL = 64
BLK = 64
TOK_G = 768
TOKENS = 12288
CAP = 1
N_DP = 16


def layout_draw(key):
    root = jax.random.fold_in(key, 7001)
    slot_map = jax.random.permutation(jax.random.fold_in(root, 1), ADAPTER_TOTAL)
    per_group = TOK_G // BLK
    owner_totals = ADAPTER_TOTAL // N_DP
    hot_owner = jax.random.randint(jax.random.fold_in(root, 2), (), 0, N_DP)

    def one_group(group_key):
        others = jax.random.permutation(jax.random.fold_in(group_key, 1), N_DP - 1)
        owner_order = jnp.concatenate([hot_owner[None], (hot_owner + 1 + others) % N_DP])
        pool = jnp.repeat(owner_order, CAP)[:per_group]
        position = jax.random.permutation(jax.random.fold_in(group_key, 2), per_group)
        owner_of = pool[position]
        choose = jax.random.randint(jax.random.fold_in(group_key, 3), (per_group,), 0, owner_totals)
        return owner_of * owner_totals + choose
    group_keys = jax.random.split(jax.random.fold_in(root, 3), N_DP)
    slots = jax.vmap(one_group)(group_keys).reshape(-1)
    inverse = jnp.argsort(slot_map)
    return (inverse[slots].astype(jnp.int32), slot_map.astype(jnp.int32))


def draw_adapter_of_block(key, part):
    return layout_draw(key)[0]


def draw_slot_of_adapter(key, part):
    return layout_draw(key)[1]


def levels(own_key, shape, pieces, smallest, largest):
    gain = 1.0
    for dim, blocks in pieces:
        steps = jax.random.uniform(jax.random.fold_in(jax.random.fold_in(own_key, 6), dim), (blocks,), jnp.float32, smallest / len(pieces), largest / len(pieces))
        gain = gain * jnp.repeat(jnp.exp(steps), shape[dim] // blocks).reshape((-1,) + (1,) * (len(shape) - 1 - dim))
    return gain


def normal_values(rng, dims, deviation, limit, cuts=(), dtype=jnp.bfloat16):
    factor_of = levels(rng, dims, cuts, -0.22, 0.18) if cuts else 1.0
    result = jax.random.normal(rng, dims, jnp.float32) * deviation * factor_of
    return jnp.minimum(jnp.maximum(result, -limit), limit).astype(dtype)


def setup_inputs(seed: int = 0) -> dict:
    streams_of = jax.random.split(jax.random.key(seed), 9)
    output_gradient = normal_values(streams_of[0], (TOKENS, MODEL_WIDTH), 1.0, 6.0, ((0, 16), (1, 32)))
    saved_gate_value = normal_values(streams_of[1], (TOKENS, HIDDEN_UNITS), 1.0, 6.0, ((0, 16), (1, 32)))
    saved_up_value = normal_values(streams_of[2], (TOKENS, HIDDEN_UNITS), 1.0, 6.0, ((0, 16), (1, 32)))
    down_weight = normal_values(streams_of[3], (HIDDEN_UNITS, MODEL_WIDTH), HIDDEN_UNITS ** -0.5, 0.046875, ((0, 32), (1, 16)))
    adapter_first_weight = normal_values(streams_of[4], (ADAPTER_TOTAL, ADAPTER_RANK, HIDDEN_UNITS), HIDDEN_UNITS ** -0.5, 0.046875, ((0, 16), (2, 32)))
    adapter_second_weight = normal_values(streams_of[5], (ADAPTER_TOTAL, ADAPTER_RANK, MODEL_WIDTH), MODEL_WIDTH ** -0.5, 0.0625, ((0, 16), (2, 32)))
    adapter_of_block = draw_adapter_of_block(jax.random.fold_in(streams_of[8], 71), 0)
    slot_of_adapter = draw_slot_of_adapter(jax.random.fold_in(streams_of[8], 71), 0)
    return {"output_gradient": output_gradient, "saved_gate_value": saved_gate_value, "saved_up_value": saved_up_value, "down_weight": down_weight, "adapter_first_weight": adapter_first_weight, "adapter_second_weight": adapter_second_weight, "adapter_of_block": adapter_of_block, "slot_of_adapter": slot_of_adapter}


adapter_scale = 2.0


def reference(output_gradient, saved_gate_value, saved_up_value, down_weight, adapter_first_weight, adapter_second_weight, adapter_of_block, slot_of_adapter):
    gate_float = saved_gate_value.astype(jnp.float32)
    up_float = saved_up_value.astype(jnp.float32)
    squash = jax.nn.sigmoid(gate_float)
    activated = gate_float * squash
    hidden = (activated * up_float).astype(jnp.bfloat16)
    block_count = adapter_of_block.shape[0]
    slot_of_block = slot_of_adapter[adapter_of_block]
    hidden_blocks = hidden.reshape(block_count, BLK, hidden.shape[1]).astype(jnp.float32)
    output_blocks = output_gradient.reshape(block_count, BLK, output_gradient.shape[1]).astype(jnp.float32)
    first_factor_blocks = adapter_first_weight[slot_of_block].astype(jnp.float32)
    second_factor_blocks = adapter_second_weight[slot_of_block].astype(jnp.float32)
    downward_factor = jnp.einsum('ntf,nrf->ntr', hidden_blocks, first_factor_blocks).astype(jnp.bfloat16)
    backward_factor = (adapter_scale * jnp.einsum('ysx,ykx->ysk', output_blocks, second_factor_blocks)).astype(jnp.bfloat16)
    side_term = jnp.einsum('ntr,nrf->ntf', backward_factor.astype(jnp.float32), first_factor_blocks).reshape(hidden.shape)
    base_term = jnp.dot(output_gradient, down_weight.T, preferred_element_type=jnp.float32)
    d_hidden = base_term + side_term
    d_gate = (d_hidden * up_float * squash * (1.0 + gate_float * (1.0 - squash))).astype(jnp.bfloat16)
    d_up = (d_hidden * activated).astype(jnp.bfloat16)
    piece_a = jnp.einsum('ntr,ntf->nrf', backward_factor.astype(jnp.float32), hidden_blocks).astype(jnp.bfloat16)
    second_factor_piece = (adapter_scale * jnp.einsum('cxh,cxe->che', downward_factor.astype(jnp.float32), output_blocks)).astype(jnp.bfloat16)
    grad_a = jax.ops.segment_sum(piece_a.astype(jnp.float32), slot_of_block, num_segments=ADAPTER_TOTAL)
    grad_b = jax.ops.segment_sum(second_factor_piece.astype(jnp.float32), slot_of_block, num_segments=ADAPTER_TOTAL)
    return d_gate, d_up, grad_a, grad_b
```

```python
import functools
import math

import jax
import jax.numpy as jnp
from jax import lax
from jax.experimental import pallas as pl
from jax.experimental.pallas import tpu as pltpu
from jax.sharding import PartitionSpec as P

BLK = 64
RANK = 64
MESH = pl.DeviceIdType.MESH
F32 = jnp.float32
BF16 = jnp.bfloat16


def dot(x, y, cx, cy):
    return lax.dot_general(x, y, (((cx,), (cy,)), ((), ())), preferred_element_type=F32)


def each(lo, hi, body):
    def step(i, carry):
        body(i)
        return carry

    lax.fori_loop(lo, hi, step, 0)


def tail_pack(x):
    return jnp.concatenate([x[:32], x[32:]], axis=1)


def tail_unpack(x):
    return jnp.concatenate([x[:, :64], x[:, 64:]], axis=0)


def kernel(
    nz, mp,
    blk_of, slot_in, slot_of, owner_of, hit_of, mask_in, og, og3, gate, up, w, a, b,
    dg, du, ga, gb,
    ogb, wb, ab, hs, hr, part, rsb, fac, bs, bb, acc, f1, f2,
    og_s, og_r, w_s, w_r, a_s, a_r, x_s, x_r, rs_s, rs_r, fg_s, fg_r, bk_s, bk_r, loc,
):
    xs = math.isqrt(mp // 2)
    ys = mp // 2 // xs
    rows, d_loc = og.shape
    nblk, _, ff = gate.shape
    own = a.shape[0]
    full = ff // 128
    half_rows = rows // 2
    g = lax.axis_index("dp")
    m = lax.axis_index("mp")

    def ring_to_mp(q):
        p, c = lax.div(q, 2), lax.rem(q, 2)
        y = lax.div(p, xs)
        x = lax.rem(lax.rem(p, xs) + ys * xs - y, xs)
        return (y * xs + x) * 2 + c

    chip = lax.div(m, 2)
    row = lax.div(chip, xs)
    q = (xs * row + lax.rem(lax.rem(chip, xs) + row, xs)) * 2 + lax.rem(m, 2)

    bar = pltpu.get_barrier_semaphore()

    def greet_z(d):
        pl.semaphore_signal(bar, inc=1, device_id=(lax.rem(g + d, nz), m), device_id_type=MESH)

    def greet_p(d):
        pl.semaphore_signal(bar, inc=1, device_id=(g, lax.rem(m + d, mp)), device_id_type=MESH)

    each(1, nz, greet_z)
    each(1, mp, greet_p)
    pl.semaphore_wait(bar, nz + mp - 2)

    class Ring:
        def __init__(self, n, pos, peer, first, buf, ssem, rsem):
            self.n, self.pos, self.peer, self.first, self.buf = n, pos, peer, first, buf
            self.ssem, self.rsem, self.size = ssem, rsem, n // 2

        def steps(self, d, h):
            return self.size if d == h else self.size - 1

        def at(self, d, s):
            return lax.rem(self.pos + (self.n - s if d == 0 else s), self.n)

        def copy(self, d, h, s, src=None):
            dst = self.buf(self.at(d, s), h)
            return pltpu.make_async_remote_copy(
                src_ref=dst if src is None else src,
                dst_ref=dst,
                send_sem=self.ssem.at[d, h, s],
                recv_sem=self.rsem.at[d, h, s],
                device_id=self.peer(lax.rem(self.pos + (1 if d == 0 else self.n - 1), self.n)),
                device_id_type=MESH,
            )

        def begin(self):
            for h in (0, 1):
                for d in (0, 1):
                    if self.steps(d, h) > 0:
                        self.copy(d, h, 0, self.first(h)).start()

        def arrived(self, d, h, s):
            ref = self.buf(self.at(d, s + 1), h)
            pltpu.make_async_remote_copy(
                src_ref=ref,
                dst_ref=ref,
                send_sem=self.ssem.at[d, h, s],
                recv_sem=self.rsem.at[d, h, s],
                device_id=self.peer(self.pos),
                device_id_type=MESH,
            ).wait_recv()

        def relay(self, s, last):
            for h in (0, 1):
                for d in (0, 1):
                    self.arrived(d, h, s - 1)
                    if d == h or not last:
                        self.copy(d, h, s).start()

        def finish(self):
            for d in (0, 1):
                self.arrived(d, d, self.size - 1)

        def sent(self):
            for h in (0, 1):
                for d in (0, 1):
                    each(0, self.steps(d, h), lambda s, d=d, h=h: self.copy(d, h, s).wait_send())

    plane = Ring(
        mp, q, lambda r: (g, ring_to_mp(r)),
        lambda h: og.at[pl.ds(h * half_rows, half_rows), :],
        lambda r, h: ogb.at[ring_to_mp(r), pl.ds(h * half_rows, half_rows), :],
        og_s, og_r,
    )
    wring = Ring(
        nz, g, lambda r: (r, m),
        lambda h: w.at[:, pl.ds(h * d_loc, d_loc)],
        lambda r, h: wb.at[r, h],
        w_s, w_r,
    )

    def some_a(r, h):
        return ab.at[pl.ds(r * own + h * (own // 2), own // 2)]

    aring = Ring(nz, g, lambda r: (r, m), lambda h: some_a(g, h), some_a, a_s, a_r)

    plane.begin()
    wring.begin()
    own_og = pltpu.make_async_copy(og, ogb.at[m], loc.at[0])
    own_og.start()

    for l in range(own):
        x = a[l].astype(F32)
        for k in range(full):
            ab[g * own + l, k * 64 : (k + 1) * 64, :] = a[l, :, k * 128 : (k + 1) * 128]
        ab[g * own + l, full * 64 :, :] = tail_pack(x[:, full * 128 :]).astype(BF16)

    def fill(o):
        at, hit = blk_of[o], hit_of[o]
        gf = gate[at].astype(F32)
        h = gf * jax.nn.sigmoid(gf) * up[at].astype(F32) * hit
        for k in range(full):
            hs[o, k * 64 : (k + 1) * 64, :] = h[:, k * 128 : (k + 1) * 128].astype(BF16)
        hs[o, full * 64 : full * 64 + 32, :] = tail_pack(h[:, full * 128 :]).astype(BF16)
        x = (og3[at].astype(F32) * hit).astype(BF16)
        for k in range(d_loc // 128):
            base = full * 64 + 32 + k * 64
            hs[o, base : base + 64, :] = x[:, k * 128 : (k + 1) * 128]

    each(0, nz, fill)
    aring.begin()

    def cross(src, dst, ssem, rsem, d):
        to = lax.rem(g + d, nz)
        return pltpu.make_async_remote_copy(
            src_ref=src.at[to], dst_ref=dst.at[g], send_sem=ssem.at[d], recv_sem=rsem.at[d],
            device_id=(to, m), device_id_type=MESH,
        )

    def crossed(dst, ssem, rsem, d):
        ref = dst.at[lax.rem(g + nz - d, nz)]
        pltpu.make_async_remote_copy(
            src_ref=ref, dst_ref=ref, send_sem=ssem.at[d], recv_sem=rsem.at[d],
            device_id=(g, m), device_id_type=MESH,
        ).wait_recv()

    each(1, nz, lambda d: cross(hs, hr, x_s, x_r, d).start())
    own_hs = pltpu.make_async_copy(hs.at[g], hr.at[g], loc.at[1])
    own_hs.start()

    acc[...] = jnp.zeros_like(acc)

    each(1, plane.size - 1, lambda s: plane.relay(s, False))
    plane.relay(plane.size - 1, True)

    plane.finish()
    own_og.wait()

    def hidden_of(j):
        parts = [hr[j, k * 64 : (k + 1) * 64, :] for k in range(full)]
        t = tail_unpack(hr[j, full * 64 : full * 64 + 32, :].astype(F32)).astype(BF16)
        return jnp.concatenate(parts + [t], axis=1)

    def grad_of(j):
        base = full * 64 + 32
        return jnp.concatenate(
            [hr[j, base + k * 64 : base + (k + 1) * 64, :] for k in range(d_loc // 128)], axis=1
        )

    def flat(src, dst, own_src, ssem, rsem, d):
        to = lax.rem(m + d, mp)
        return pltpu.make_async_remote_copy(
            src_ref=src.at[m if own_src else to], dst_ref=dst.at[m],
            send_sem=ssem.at[d], recv_sem=rsem.at[d], device_id=(g, to), device_id_type=MESH,
        )

    def flat_arrived(dst, ssem, rsem, d):
        ref = dst.at[lax.rem(m + mp - d, mp)]
        pltpu.make_async_remote_copy(
            src_ref=ref, dst_ref=ref, send_sem=ssem.at[d], recv_sem=rsem.at[d],
            device_id=(g, m), device_id_type=MESH,
        ).wait_recv()

    def stage_partial():
        own_hs.wait()
        each(1, nz, lambda d: crossed(hr, x_s, x_r, d))

        def one(j):
            idx = slot_in[j]
            down = dot(hidden_of(j), a[idx], 1, 1)
            back = dot(grad_of(j), b[idx], 1, 1)
            both = jnp.concatenate([down, back], axis=1)
            part[2 * j] = both[:32]
            part[2 * j + 1] = both[32:]

        each(0, nz, one)
        each(1, mp, lambda d: flat(part, rsb, False, rs_s, rs_r, d).start())

    lane = lax.broadcasted_iota(jnp.int32, (32, 128), 1)

    def stage_sum():
        rsb[m] = part[m]
        each(1, mp, lambda d: flat_arrived(rsb, rs_s, rs_r, d))
        total = lax.fori_loop(0, mp, lambda c, t: t + rsb[c], jnp.zeros((32, 128), F32))
        fac[m] = jnp.where(lane < 64, total, 2.0 * total).astype(BF16)
        each(1, mp, lambda d: flat(fac, fac, True, fg_s, fg_r, d).start())

    def stage_back():
        each(1, mp, lambda d: flat_arrived(fac, fg_s, fg_r, d))

        def one(j):
            top = pltpu.roll(fac[2 * j].astype(F32), 64, 1)
            bs[j] = jnp.where(lane < 64, top, fac[2 * j + 1].astype(F32)).astype(BF16)

        each(0, nz, one)
        bb[g] = bs[g]
        each(1, nz, lambda d: cross(bs, bb, bk_s, bk_r, d).start())

    def stage_grads():
        ga[...] = jnp.zeros_like(ga)
        gb[...] = jnp.zeros_like(gb)

        def one(j):
            f = jnp.concatenate([fac[2 * j], fac[2 * j + 1]], axis=0)
            pa = dot(f, hidden_of(j), 0, 0)[64:].astype(BF16).astype(F32)
            pb = (2.0 * dot(f, grad_of(j), 0, 0)[:64]).astype(BF16).astype(F32)
            for l in range(own):
                ga[l] += pa * mask_in[j * own + l]
                gb[l] += pb * mask_in[j * own + l]

        each(0, nz, one)

    def stage_gate():
        def one(k):
            r = pl.ds(pl.multiple_of(k * BLK, BLK), BLK)
            gf = gate[k].astype(F32)
            uf = up[k].astype(F32)
            s = jax.nn.sigmoid(gf)
            f1[r, :] = uf * s * (1.0 + gf * (1.0 - s))
            f2[r, :] = gf * s

        each(0, nblk, one)

    def stage_side():
        each(1, nz, lambda d: crossed(bb, bk_s, bk_r, d))

        def one(k):
            p = ab[slot_of[k]]
            t = tail_unpack(p[full * 64 :].astype(F32)).astype(BF16)
            first = jnp.concatenate([p[i * 64 : (i + 1) * 64] for i in range(full)] + [t], axis=1)
            back = tail_unpack(bb[owner_of[k]].astype(F32)).astype(BF16)
            r = pl.ds(pl.multiple_of(k * BLK, BLK), BLK)
            acc[r, :] += dot(back, first, 1, 0)

        each(0, nblk, one)

    tile = rows // 3

    def multiply(z, h, wref):
        for t in range(3):
            r = pl.ds(t * tile, tile)
            acc[r, :] += dot(ogb[2 * z + h, r, :], wref, 1, 1)

    def own_w():
        for h in (0, 1):
            multiply(g, h, w[:, h * d_loc : (h + 1) * d_loc])

    def multiply_step(s):
        def one(c):
            d, h = lax.div(c, 2), lax.rem(c, 2)
            z = lax.rem(g + jnp.where(d == 0, nz - s, s), nz)
            multiply(z, h, wb[z, h])

        each(0, 4, one)

    stages = [stage_partial, stage_sum, stage_back, stage_grads, stage_gate, stage_side]
    asteps = list(range(1, aring.size))
    done = [False]

    def relay_a():
        if asteps:
            s = asteps.pop(0)
            aring.relay(s, s == aring.size - 1)
        elif not done[0]:
            done[0] = True
            aring.finish()

    for s in range(1, wring.size):
        relay_a()
        wring.relay(s, s == wring.size - 1)
        relay_a()
        if s == 1:
            own_w()
        multiply_step(s)
        if len(stages) > 1 or (stages and done[0]):
            stages.pop(0)()
    while not done[0]:
        relay_a()
    for stage in stages:
        stage()
    wring.finish()

    def last(c):
        z = lax.rem(g + nz // 2, nz)
        multiply(z, c, wb[z, c])

    each(0, 2, last)

    def out(k):
        r = pl.ds(pl.multiple_of(k * BLK, BLK), BLK)
        x = acc[r, :]
        dg[r, :] = (x * f1[r, :]).astype(BF16)
        du[r, :] = (x * f2[r, :]).astype(BF16)

    each(0, nblk, out)

    plane.sent()
    wring.sent()
    aring.sent()
    each(1, nz, lambda d: cross(hs, hr, x_s, x_r, d).wait_send())
    each(1, mp, lambda d: flat(part, rsb, False, rs_s, rs_r, d).wait_send())
    each(1, mp, lambda d: flat(fac, fac, True, fg_s, fg_r, d).wait_send())
    each(1, nz, lambda d: cross(bs, bb, bk_s, bk_r, d).wait_send())


def shards(og, gate, up, w, a, b, aob, soa):
    nz, mp = lax.axis_size("dp"), lax.axis_size("mp")
    rows, d_loc = og.shape
    ff = gate.shape[1]
    own = a.shape[0]
    nblk = rows // BLK
    g = lax.axis_index("dp")
    match = aob[:, None] == jnp.arange(soa.shape[0], dtype=jnp.int32)[None, :]
    slot = jnp.sum(jnp.where(match, soa[None, :], 0), axis=1).reshape(nz, nblk)
    owner = slot // own
    mine = lax.dynamic_index_in_dim(owner, g, 0, keepdims=False)
    slot_of = lax.dynamic_index_in_dim(slot, g, 0, keepdims=False)
    to_owner = mine[None, :] == jnp.arange(nz, dtype=jnp.int32)[:, None]
    blk_of = jnp.sum(jnp.where(to_owner, jnp.arange(nblk, dtype=jnp.int32)[None, :], 0), axis=1)
    hit_of = jnp.sum(to_owner.astype(F32), axis=1)
    here = owner == g
    slot_in = jnp.sum(jnp.where(here, slot % own, 0), axis=1)
    is_slot = here[:, None, :] & (
        (slot % own)[:, None, :] == jnp.arange(own, dtype=jnp.int32)[None, :, None]
    )
    mask_in = jnp.sum(is_slot.astype(F32), axis=2).reshape(nz * own)
    packed = ff * 64 // 128
    send = (ff + d_loc) * 64 // 128
    vm = pl.BlockSpec(memory_space=pltpu.VMEM)
    sm = pl.BlockSpec(memory_space=pltpu.SMEM)
    dma = pltpu.SemaphoreType.DMA
    return pl.pallas_call(
        functools.partial(kernel, nz, mp),
        out_shape=(
            jax.ShapeDtypeStruct((rows, ff), BF16),
            jax.ShapeDtypeStruct((rows, ff), BF16),
            jax.ShapeDtypeStruct((own, RANK, ff), F32),
            jax.ShapeDtypeStruct((own, RANK, d_loc), F32),
        ),
        in_specs=[sm] * 6 + [vm] * 7,
        out_specs=(vm,) * 4,
        scratch_shapes=[
            pltpu.VMEM((mp, rows, d_loc), BF16),
            pltpu.VMEM((nz, 2, ff, d_loc), BF16),
            pltpu.VMEM((nz * own, packed, 128), BF16),
            pltpu.VMEM((nz, send, 128), BF16),
            pltpu.VMEM((nz, send, 128), BF16),
            pltpu.VMEM((mp, 32, 128), F32),
            pltpu.VMEM((mp, 32, 128), F32),
            pltpu.VMEM((mp, 32, 128), BF16),
            pltpu.VMEM((nz, 32, 128), BF16),
            pltpu.VMEM((nz, 32, 128), BF16),
            pltpu.VMEM((rows, ff), F32),
            pltpu.VMEM((rows, ff), F32),
            pltpu.VMEM((rows, ff), F32),
            dma((2, 2, mp // 2)), dma((2, 2, mp // 2)),
            dma((2, 2, nz // 2)), dma((2, 2, nz // 2)),
            dma((2, 2, nz // 2)), dma((2, 2, nz // 2)),
            dma((nz,)), dma((nz,)),
            dma((mp,)), dma((mp,)),
            dma((mp,)), dma((mp,)),
            dma((nz,)), dma((nz,)),
            dma((2,)),
        ],
        compiler_params=pltpu.CompilerParams(
            collective_id=0, has_side_effects=True, vmem_limit_bytes=60 * 1024 * 1024
        ),
    )(
        blk_of, slot_in, slot_of, mine, hit_of, mask_in, og, og.reshape(nblk, BLK, d_loc),
        gate.reshape(nblk, BLK, ff), up.reshape(nblk, BLK, ff), w, a, b,
    )


def solution(mesh):
    in_specs = (
        P("dp", "mp"),
        P("dp", "mp"),
        P("dp", "mp"),
        P("mp", "dp"),
        P("dp", None, "mp"),
        P("dp", None, "mp"),
        P(),
        P(),
    )
    out_specs = (P("dp", "mp"), P("dp", "mp"), P("dp", None, "mp"), P("dp", None, "mp"))
    return jax.shard_map(shards, mesh=mesh, in_specs=in_specs, out_specs=out_specs, check_vma=False)
```

```python
import functools
import math

import jax
import jax.numpy as jnp
from jax import lax
from jax.experimental import pallas as pl
from jax.experimental.pallas import tpu as pltpu
from jax.sharding import PartitionSpec as P

BLK = 64
RANK = 64
MESH = pl.DeviceIdType.MESH
F32 = jnp.float32
BF16 = jnp.bfloat16


def dot(x, y, cx, cy):
    return lax.dot_general(x, y, (((cx,), (cy,)), ((), ())), preferred_element_type=F32)


def each(lo, hi, body):
    def step(i, carry):
        body(i)
        return carry

    if hi > lo:
        lax.fori_loop(lo, hi, step, 0)


def same(x, y):
    return 1 - jnp.minimum(jnp.abs(x - y), 1)


def swap(x):
    return pltpu.roll(x, 64, 1)


def kernel(
    nz, mp,
    aob, soa, og, og3, gate, up, w, a, b,
    out, ga, gb,
    ogb, wb, ab, asel, apk, asend, og3v, gv, uv, av, bv, hp, hs, hr, xb, part, rsb, fac, bk1, bk2, gap,
    blk_of, hit_of, slot_in, mask_in, a_at, sel_at, sel_of, owner_of,
    og_s, og_r, w_s, w_r, a_s, a_r, x_s, x_r, rs_s, rs_r, fg_s, fg_r, bk_s, bk_r, bc_s, bc_r,
    sl_s, sl_r, xb_s, xb_r, loc, tok,
):
    xs = math.isqrt(mp // 2)
    ys = mp // 2 // xs
    rows, d_loc = og.shape
    ff = gate.shape[0]
    nblk = rows // BLK
    own = a.shape[0]
    half_rows = rows // 2
    fh = ff // 2
    units = nz * 8 // mp
    tail = min(3, nz // 2 - 1)
    reach = (nz // 2 - tail, nz // 2 - 1 - tail)
    quarter = nz // 4
    mid = (fh + d_loc // 2) // 2
    g = lax.axis_index("dp")
    m = lax.axis_index("mp")
    sign = 1 - 2 * lax.rem(m, 2)

    def ring_to_mp(q):
        p, c = lax.div(q, 2), lax.rem(q, 2)
        y = lax.div(p, xs)
        x = lax.rem(lax.rem(p, xs) + ys * xs - y, xs)
        return (y * xs + x) * 2 + c

    chip = lax.div(m, 2)
    row = lax.div(chip, xs)
    q = (xs * row + lax.rem(lax.rem(chip, xs) + row, xs)) * 2 + lax.rem(m, 2)

    def wrap(r):
        return lax.rem(r + 2 * nz, nz)

    def local(src, dst, k):
        return pltpu.make_async_copy(src, dst, loc.at[k])

    locals_ = [
        local(a, av, 0), local(gate, gv, 1), local(up, uv, 2), local(og3, og3v, 3),
        local(b, bv, 4), local(og, ogb.at[m], 5),
        local(w.at[:, pl.ds(0, d_loc)], wb.at[g, 0], 6),
        local(w.at[:, pl.ds(d_loc, d_loc)], wb.at[g, 1], 7),
    ]
    for c in locals_:
        c.start()

    bar = pltpu.get_barrier_semaphore()
    for d in (1, nz - 1):
        pl.semaphore_signal(bar, inc=1, device_id=(wrap(g + d), m), device_id_type=MESH)
    for d in (1, mp - 1):
        pl.semaphore_signal(
            bar, inc=1, device_id=(g, ring_to_mp(lax.rem(q + d, mp))), device_id_type=MESH
        )
    pl.semaphore_wait(bar, 4)

    known = nz // 2 - 1

    def token(d):
        pl.semaphore_signal(
            tok.at[d], inc=1, device_id=(wrap(g + (1 if d == 0 else -1)), m), device_id_type=MESH
        )

    def pass_tokens():
        for d in (0, 1):
            pl.semaphore_wait(tok.at[d], 1)
            token(d)

    class Ring:
        def __init__(self, n, pos, sign, counts, peer, first, buf, ssem, rsem):
            self.n, self.pos, self.sign, self.counts = n, pos, sign, counts
            self.peer, self.first, self.buf, self.ssem, self.rsem = peer, first, buf, ssem, rsem
            self.size = max(max(c) for c in counts)

        def at(self, d, s):
            step = self.sign * s if d == 0 else -self.sign * s
            return lax.rem(self.pos + 2 * self.n - step, self.n)

        def copy(self, d, h, s, src=None):
            dst = self.buf(self.at(d, s), h)
            return pltpu.make_async_remote_copy(
                src_ref=dst if src is None else src,
                dst_ref=dst,
                send_sem=self.ssem.at[d, h, s],
                recv_sem=self.rsem.at[d, h, s],
                device_id=self.peer(self.at(d, -1)),
                device_id_type=MESH,
            )

        def begin(self):
            for h in (0, 1):
                for d in (0, 1):
                    if self.counts[d][h] > 0:
                        self.copy(d, h, 0, self.first(h)).start()

        def arrived(self, d, h, s):
            ref = self.buf(self.at(d, s + 1), h)
            pltpu.make_async_remote_copy(
                src_ref=ref,
                dst_ref=ref,
                send_sem=self.ssem.at[d, h, s],
                recv_sem=self.rsem.at[d, h, s],
                device_id=self.peer(self.pos),
                device_id_type=MESH,
            ).wait_recv()

        def relay(self, s, k=None):
            k = s if k is None else k
            for h in (0, 1):
                for d in (0, 1):
                    if k - 1 < self.counts[d][h]:
                        self.arrived(d, h, s - 1)
                    if k < self.counts[d][h]:
                        self.copy(d, h, s).start()

        def sent(self):
            for h in (0, 1):
                for d in (0, 1):
                    each(
                        0, self.counts[d][h],
                        lambda s, d=d, h=h: self.copy(d, h, s).wait_send(),
                    )

    def halves(n):
        return ((n // 2, n // 2 - 1), (n // 2 - 1, n // 2))

    plane = Ring(
        mp, q, 1, halves(mp), lambda r: (g, ring_to_mp(r)),
        lambda h: og.at[pl.ds(h * half_rows, half_rows), :],
        lambda r, h: ogb.at[ring_to_mp(r), pl.ds(h * half_rows, half_rows), :],
        og_s, og_r,
    )
    wring = Ring(
        nz, g, 1, halves(nz), lambda r: (r, m),
        lambda h: w.at[:, pl.ds(h * d_loc, d_loc)],
        lambda r, h: wb.at[r, h],
        w_s, w_r,
    )

    def some_a(r, h):
        return ab.at[pl.ds(r * own + h * (own // 2), own // 2)]

    aring = Ring(
        nz, g, sign, tuple((r, r) for r in reach), lambda r: (r, m),
        lambda h: apk.at[pl.ds(h * (own // 2), own // 2)], some_a, a_s, a_r,
    )

    wring.begin()
    plane.begin()
    for d in (0, 1):
        token(d)

    lane = lax.broadcasted_iota(jnp.int32, (fh, 128), 1)
    lane64 = lax.broadcasted_iota(jnp.int32, (RANK, 128), 1)

    locals_[0].wait()
    eye = (
        lax.broadcasted_iota(jnp.int32, (RANK, 128), 0) == lane64
    ).astype(F32).astype(BF16)
    for l in range(own):
        t = dot(av[l], eye, 0, 0)
        t = jnp.where(lane < 64, t[:fh], swap(t[fh:])).astype(BF16)
        apk[l] = t
        ab[g * own + l] = t
    aring.begin()

    slots = [soa[aob[g * nblk + k]] for k in range(nblk)]
    owners = [lax.div(s, own) for s in slots]

    def block_for(o):
        at, hit = jnp.int32(0), jnp.int32(0)
        for k in range(nblk):
            e = same(owners[k], o)
            at, hit = at + k * e, hit + e
        blk_of[o] = jnp.minimum(at, nblk - 1)
        hit_of[o] = hit.astype(F32)

    each(0, nz, block_for)

    locals_[1].wait()
    locals_[2].wait()

    def tile_of(j):
        c = pl.ds(pl.multiple_of(j * 128, 128), 128)
        gf = gv[:, c].astype(F32)
        h = gf * jax.nn.sigmoid(gf) * uv[:, c].astype(F32)
        hp[2 * j] = jnp.where(lane < 64, h[:fh], swap(h[fh:])).astype(BF16)
        hp[2 * j + 1] = jnp.where(lane < 64, swap(h[:fh]), h[fh:]).astype(BF16)

    both = min(known - 1, nblk // 2)

    def tile_and_token(j):
        tile_of(j)
        pass_tokens()

    each(0, both, tile_and_token)
    each(both, nblk // 2, tile_of)
    locals_[3].wait()

    def fill(o):
        at, hit = blk_of[o], hit_of[o]
        hs[o, :fh] = (hp[at].astype(F32) * hit).astype(BF16)
        x = (og3v[at].astype(F32) * hit).astype(BF16)
        for k in range(d_loc // 128):
            hs[o, fh + k * 64 : fh + (k + 1) * 64] = x[:, k * 128 : (k + 1) * 128]

    each(0, nz, fill)
    each(both, known - 1, lambda j: pass_tokens())
    for d in (0, 1):
        pl.semaphore_wait(tok.at[d], 1)

    def remote(src, dst, ssem, rsem, z, p):
        return pltpu.make_async_remote_copy(
            src_ref=src, dst_ref=dst, send_sem=ssem, recv_sem=rsem,
            device_id=(z, p), device_id_type=MESH,
        )

    far = wrap(g + nz // 2)

    def piece(ref, i):
        return ref.at[pl.ds(i * mid, mid)]

    def leg1(i):
        to = wrap(g + (quarter if i == 0 else -quarter))
        return remote(piece(hs.at[far], i), xb.at[i], xb_s.at[0, i], xb_r.at[0, i], to, m)

    def leg2(i):
        d = quarter if i == 0 else -quarter
        dst = piece(hr.at[wrap(g - d)], i)
        return remote(xb.at[i], dst, xb_s.at[1, i], xb_r.at[1, i], wrap(g + d), m)

    def leg2_in(i):
        ref = piece(hr.at[far], i)
        return remote(ref, ref, xb_s.at[1, i], xb_r.at[1, i], g, m)

    def block_copy(d):
        to = wrap(g + d)
        return remote(hs.at[to], hr.at[g], x_s.at[d], x_r.at[d], to, m)

    def block_in(d):
        ref = hr.at[wrap(g - d)]
        remote(ref, ref, x_s.at[d], x_r.at[d], g, m).wait_recv()

    def others(body):
        each(1, nz // 2, body)
        each(nz // 2 + 1, nz, body)

    for i in (0, 1):
        leg1(i).start()
    others(lambda d: block_copy(d).start())
    own_hs = local(hs.at[g], hr.at[g], 8)
    own_hs.start()

    def group_tables(j):
        hit, at = jnp.int32(0), jnp.int32(0)
        for k in range(nblk):
            s = soa[aob[j * nblk + k]]
            e = same(lax.div(s, own), g)
            hit, at = hit + e, at + e * lax.rem(s, own)
        slot_in[j] = jnp.minimum(at, own - 1)
        for l in range(own):
            mask_in[j * own + l] = (hit * same(at, l)).astype(F32)

    each(0, nz, group_tables)
    for k in range(nblk):
        o = owners[k]
        dist = lax.rem(sign * (g - o) + nz, nz)
        picked = jnp.minimum(jnp.maximum(dist - reach[0], 0), 1) * jnp.minimum(
            jnp.maximum(nz - reach[1] - dist, 0), 1
        )
        a_at[k] = picked * (g * own) + (1 - picked) * slots[k]
        sel_at[k] = picked * o + (1 - picked) * wrap(g - sign * (reach[0] + 1))
        sel_of[k] = picked.astype(F32)
        owner_of[k] = o

    turn = min(6, plane.size - 1)
    each(1, turn, lambda s: plane.relay(s, 1))
    for i in (0, 1):
        remote(xb.at[i], xb.at[i], xb_s.at[0, i], xb_r.at[0, i], g, m).wait_recv()
        leg2(i).start()
    each(turn, plane.size - 1, lambda s: plane.relay(s, 1))
    plane.relay(plane.size - 1)
    plane.relay(plane.size)
    for c in locals_[4:]:
        c.wait()

    def grad_tile(j, k):
        return hr[j, fh + k * 64 : fh + (k + 1) * 64]

    def rows_of(ref, p):
        return ref.at[pl.ds(units * lax.div(p, 8), units), lax.rem(p, 8)]

    def part_copy(d):
        to = lax.rem(m + d, mp)
        return remote(rows_of(part, to), rsb.at[m], rs_s.at[d], rs_r.at[d], g, to)

    def part_in(d):
        ref = rsb.at[lax.rem(m + mp - d, mp)]
        remote(ref, ref, rs_s.at[d], rs_r.at[d], g, m).wait_recv()

    def fac_copy(d):
        to = lax.rem(m + d, mp)
        return remote(rows_of(fac, m), rows_of(fac, m), fg_s.at[d], fg_r.at[d], g, to)

    def fac_in(d):
        ref = rows_of(fac, lax.rem(m + mp - d, mp))
        remote(ref, ref, fg_s.at[d], fg_r.at[d], g, m).wait_recv()

    my_units = units * lax.div(m, 8)
    my_row = lax.rem(m, 8)

    def stage_partial():
        own_hs.wait()
        others(block_in)
        for i in (0, 1):
            leg2_in(i).wait_recv()

        def one(j):
            l = slot_in[j]
            z = dot(apk[l], hr[j, :fh], 0, 0)
            down = z[:64] + swap(z[64:])
            back = jnp.zeros((RANK, BLK), F32)
            for k in range(d_loc // 128):
                back += dot(bv[l, :, k * 128 : (k + 1) * 128], grad_tile(j, k), 1, 1)
            both = jnp.concatenate([down[:, :64], back], axis=1)
            part[j] = both.reshape(8, 8, 128)

        each(0, nz, one)
        each(1, mp, lambda d: part_copy(d).start())

    def stage_sum():
        rsb[m] = part[pl.ds(my_units, units), my_row]
        each(1, mp, part_in)
        total = lax.fori_loop(
            0, mp, lambda c, t: t + rsb[c], jnp.zeros((units, 8, 128), F32)
        )
        left = lax.broadcasted_iota(jnp.int32, (units, 8, 128), 2) < 64
        total = jnp.where(left, total, 2.0 * total).astype(BF16).astype(F32)
        fac[pl.ds(my_units, units), my_row] = total
        each(1, mp, lambda d: fac_copy(d).start())

    def back_copy(i):
        to = my_units + i
        return remote(fac.at[to, my_row], bk1.at[g], bk_s.at[i], bk_r.at[g], to, m)

    def back_in(o):
        remote(bk1.at[o], bk1.at[o], bk_s.at[0], bk_r.at[o], g, m).wait_recv()

    def stage_back():
        each(1, mp, fac_in)
        for i in range(units):
            @pl.when(my_units + i == g)
            def _():
                bk1[g] = fac[g, my_row]

            @pl.when(my_units + i != g)
            def _():
                back_copy(i).start()

    team = lax.div(g, units)

    def share_copy(d):
        to = lax.rem(m + d, mp)
        return remote(bk1, bk2.at[:, my_row], bc_s.at[d], bc_r.at[my_row], g, to)

    def stage_share():
        @pl.when(lax.div(m, 8) == team)
        def _():
            each(1, nz, lambda d: back_in(wrap(g + d)))
            each(1, mp, lambda d: share_copy(d).start())

    def stage_grads():
        gap[...] = jnp.zeros_like(gap)
        gb[...] = jnp.zeros_like(gb)

        def one(j):
            f = fac[j].reshape(RANK, 128)
            top = jnp.where(lane64 < 64, swap(f), 0.0).astype(BF16)
            bot = jnp.where(lane64 < 64, 0.0, f).astype(BF16)
            pa = dot(jnp.concatenate([top, bot], axis=0), hr[j, :fh], 1, 1)
            pa = pa.astype(BF16).astype(F32)
            down = f.astype(BF16)[:, :64]
            for k in range(d_loc // 128):
                c = slice(k * 128, (k + 1) * 128)
                pb = (2.0 * dot(down, grad_tile(j, k), 1, 0)).astype(BF16).astype(F32)
                for l in range(own):
                    gb[l, :, c] += pb * mask_in[j * own + l]
            for l in range(own):
                gap[l] += pa * mask_in[j * own + l]

        each(0, nz, one)
        for l in range(own):
            ga[l] = jnp.concatenate([gap[l, :64], gap[l, 64:]], axis=1)

    def picks():
        return ((0, wrap(g - sign * reach[0]), sign), (1, wrap(g + sign * reach[1]), -sign))

    def pick_copy(d, o, step, k):
        to = wrap(g + step * k)
        return remote(
            asend.at[d * 3 + k - 1], asel.at[o], sl_s.at[d, k - 1], sl_r.at[d, k - 1], to, m
        )

    def pick_send():
        for d, o, step in picks():
            for k in range(1, tail + 1):
                to = wrap(g + step * k)
                at = jnp.int32(0)
                for i in range(nblk):
                    s = soa[aob[to * nblk + i]]
                    at = at + same(lax.div(s, own), o) * lax.rem(s, own)
                asend[d * 3 + k - 1] = ab[o * own + jnp.minimum(at, own - 1)]
        for d, o, step in picks():
            for k in range(1, tail + 1):
                pick_copy(d, o, step, k).start()

    def pick_in():
        for k in range(1, tail + 1):
            for d, o in ((0, wrap(g - sign * (reach[0] + k))), (1, wrap(g + sign * (reach[1] + k)))):
                ref = asel.at[o]
                remote(ref, ref, sl_s.at[d, k - 1], sl_r.at[d, k - 1], g, m).wait_recv()

    def stage_side():
        pick_in()

        def row_in(t):
            ref = bk2.at[:, t]

            @pl.when(units_first + t != m)
            def _():
                remote(ref, ref, bc_s.at[0], bc_r.at[t], g, m).wait_recv()

        units_first = 8 * team

        @pl.when(lax.div(m, 8) == team)
        def _():
            bk2[:, my_row] = bk1[...]

        each(0, 8, row_in)

        def first_of(k):
            near, sel = ab[a_at[k]].astype(F32), asel[sel_at[k]].astype(F32)
            return near * (1.0 - sel_of[k]) + sel * sel_of[k]

        def one(j):
            a1, a2 = first_of(2 * j), first_of(2 * j + 1)
            top = jnp.where(lane < 64, a1, swap(a2)).astype(BF16)
            bot = jnp.where(lane < 64, swap(a1), a2).astype(BF16)
            b1 = bk2[owner_of[2 * j]].reshape(RANK, 128)
            b2 = bk2[owner_of[2 * j + 1]].reshape(RANK, 128)
            r = jnp.concatenate(
                [jnp.where(lane64 < 64, swap(b1), 0.0), jnp.where(lane64 < 64, 0.0, b2)], axis=0
            ).astype(BF16)
            c = pl.ds(pl.multiple_of(j * 128, 128), 128)
            out[:fh, c] += dot(top, r, 1, 0)
            out[fh:, c] += dot(bot, r, 1, 0)

        each(0, nblk // 2, one)

    tile = 256 if rows % 256 == 0 else 128

    def multiply(z, h, fresh=False):
        x = wb[z, h]
        for t in range(rows // tile):
            c = slice(t * tile, (t + 1) * tile)
            y = dot(x, ogb[2 * z + h, c, :], 1, 1)
            if fresh:
                out[:, c] = y
            else:
                out[:, c] += y

    def multiply_step(s):
        def one(c):
            d, h = lax.div(c, 2), lax.rem(c, 2)
            multiply(wrap(g + (2 * d - 1) * s), h)

        each(0, 4, one)

    stages = [stage_partial, stage_sum, stage_back, stage_share, stage_grads, stage_side]
    a_steps = [functools.partial(aring.relay, s) for s in range(1, reach[0] + 1)] + [pick_send]
    for s in range(1, nz // 2):
        if a_steps:
            a_steps.pop(0)()
        wring.relay(s)
        if a_steps:
            a_steps.pop(0)()
        if s == 1:
            multiply(g, 0, True)
            multiply(g, 1)
        multiply_step(s)
        if stages and (len(stages) > 1 or not a_steps):
            stages.pop(0)()
    for f in a_steps + stages:
        f()
    wring.relay(nz // 2)
    each(0, 2, lambda c: multiply(far, c))

    plane.sent()
    wring.sent()
    aring.sent()
    others(lambda d: block_copy(d).wait_send())
    for i in (0, 1):
        leg1(i).wait_send()
        leg2(i).wait_send()
    each(1, mp, lambda d: part_copy(d).wait_send())
    each(1, mp, lambda d: fac_copy(d).wait_send())
    for i in range(units):
        @pl.when(my_units + i != g)
        def _():
            back_copy(i).wait_send()

    @pl.when(lax.div(m, 8) == team)
    def _():
        each(1, mp, lambda d: share_copy(d).wait_send())

    for d, o, step in picks():
        for k in range(1, tail + 1):
            pick_copy(d, o, step, k).wait_send()


def shards(og, gate, up, w, a, b, aob, soa):
    nz, mp = lax.axis_size("dp"), lax.axis_size("mp")
    rows, d_loc = og.shape
    ff = gate.shape[1]
    own = a.shape[0]
    nblk = rows // BLK
    fh = ff // 2
    send = fh + d_loc // 2
    units = nz * 8 // mp
    gate, up = gate.T, up.T
    vm = pl.BlockSpec(memory_space=pltpu.VMEM)
    sm = pl.BlockSpec(memory_space=pltpu.SMEM)
    hbm = pl.BlockSpec(memory_space=pl.ANY)
    dma = pltpu.SemaphoreType.DMA
    d_hidden, ga, gb = pl.pallas_call(
        functools.partial(kernel, nz, mp),
        out_shape=(
            jax.ShapeDtypeStruct((ff, rows), F32),
            jax.ShapeDtypeStruct((own, RANK, ff), F32),
            jax.ShapeDtypeStruct((own, RANK, d_loc), F32),
        ),
        in_specs=[sm] * 2 + [hbm] * 7,
        out_specs=(vm,) * 3,
        scratch_shapes=[
            pltpu.VMEM((mp, rows, d_loc), BF16),
            pltpu.VMEM((nz, 2, ff, d_loc), BF16),
            pltpu.VMEM((nz * own, fh, 128), BF16),
            pltpu.VMEM((nz, fh, 128), BF16),
            pltpu.VMEM((own, fh, 128), BF16),
            pltpu.VMEM((6, fh, 128), BF16),
            pltpu.VMEM((nblk, BLK, d_loc), BF16),
            pltpu.VMEM((ff, rows), BF16),
            pltpu.VMEM((ff, rows), BF16),
            pltpu.VMEM((own, RANK, ff), BF16),
            pltpu.VMEM((own, RANK, d_loc), BF16),
            pltpu.VMEM((nblk, fh, 128), BF16),
            pltpu.VMEM((nz, send, 128), BF16),
            pltpu.VMEM((nz, send, 128), BF16),
            pltpu.VMEM((2, send // 2, 128), BF16),
            pltpu.VMEM((nz, 8, 8, 128), F32),
            pltpu.VMEM((mp, units, 8, 128), F32),
            pltpu.VMEM((nz, 8, 8, 128), F32),
            pltpu.VMEM((nz, 8, 128), F32),
            pltpu.VMEM((nz, 8, 8, 128), F32),
            pltpu.VMEM((own, 2 * RANK, fh), F32),
            pltpu.SMEM((nz,), jnp.int32),
            pltpu.SMEM((nz,), F32),
            pltpu.SMEM((nz,), jnp.int32),
            pltpu.SMEM((nz * own,), F32),
            pltpu.SMEM((nblk,), jnp.int32),
            pltpu.SMEM((nblk,), jnp.int32),
            pltpu.SMEM((nblk,), F32),
            pltpu.SMEM((nblk,), jnp.int32),
            dma((2, 2, mp // 2)), dma((2, 2, mp // 2)),
            dma((2, 2, nz // 2)), dma((2, 2, nz // 2)),
            dma((2, 2, nz // 2)), dma((2, 2, nz // 2)),
            dma((nz,)), dma((nz,)),
            dma((mp,)), dma((mp,)),
            dma((mp,)), dma((mp,)),
            dma((units,)), dma((nz,)),
            dma((mp,)), dma((8,)),
            dma((2, 3)), dma((2, 3)),
            dma((2, 2)), dma((2, 2)),
            dma((9,)),
            pltpu.SemaphoreType.REGULAR((2,)),
        ],
        compiler_params=pltpu.CompilerParams(
            collective_id=0, has_side_effects=True, vmem_limit_bytes=48 * 1024 * 1024
        ),
    )(aob, soa, og, og.reshape(nblk, BLK, d_loc), gate, up, w, a, b)
    gf, uf = gate.astype(F32), up.astype(F32)
    s = jax.nn.sigmoid(gf)
    d_gate = (d_hidden * uf * s * (1.0 + gf * (1.0 - s))).astype(BF16)
    d_up = (d_hidden * (gf * s)).astype(BF16)
    return d_gate.T, d_up.T, ga, gb


def solution(mesh):
    in_specs = (
        P("dp", "mp"),
        P("dp", "mp"),
        P("dp", "mp"),
        P("mp", "dp"),
        P("dp", None, "mp"),
        P("dp", None, "mp"),
        P(),
        P(),
    )
    out_specs = (P("dp", "mp"), P("dp", "mp"), P("dp", None, "mp"), P("dp", None, "mp"))
    return jax.shard_map(shards, mesh=mesh, in_specs=in_specs, out_specs=out_specs, check_vma=False)
```

```python
import functools
import math

import jax
import jax.numpy as jnp
from jax import lax
from jax.experimental import pallas as pl
from jax.experimental.pallas import tpu as pltpu
from jax.sharding import PartitionSpec as P

BLK = 64
RANK = 64
MESH = pl.DeviceIdType.MESH
F32 = jnp.float32
BF16 = jnp.bfloat16


def dot(x, y, cx, cy):
    return lax.dot_general(x, y, (((cx,), (cy,)), ((), ())), preferred_element_type=F32)


def each(lo, hi, body):
    def step(i, carry):
        body(i)
        return carry

    if hi > lo:
        lax.fori_loop(lo, hi, step, 0)


def same(x, y):
    return 1 - jnp.minimum(jnp.abs(x - y), 1)


def swap(x):
    return pltpu.roll(x, 64, 1)


def kernel(
    nz, mp,
    aob, soa, og, og3, gate, up, w, a, b,
    out, ga, gb,
    ogb, wb, ab, asel, apk, asend, og3v, gv, uv, av, bv, hp, hs, hr, xb, part, rsb, fac, bk1, shs, bk2, gap,
    blk_of, hit_of, slot_in, mask_in, a_at, sel_at, sel_of, quad_of, half_of, odd_of,
    og_s, og_r, w_s, w_r, a_s, a_r, x_s, x_r, rs_s, rs_r, fg_s, fg_r, bk_s, bk_r, bc_s, bc_r,
    sl_s, sl_r, xb_s, xb_r, loc, tok,
):
    xs = math.isqrt(mp // 2)
    ys = mp // 2 // xs
    rows, d_loc = og.shape
    ff = gate.shape[0]
    nblk = rows // BLK
    own = a.shape[0]
    half_rows = rows // 2
    fh = ff // 2
    units = nz * 8 // mp
    tail = min(3, nz // 2 - 1)
    reach = (nz // 2 - tail, nz // 2 - 1 - tail)
    quarter = nz // 4
    mid = (fh + d_loc // 2) // 2
    g = lax.axis_index("dp")
    m = lax.axis_index("mp")
    sign = 1 - 2 * lax.rem(m, 2)

    def ring_to_mp(q):
        p, c = lax.div(q, 2), lax.rem(q, 2)
        y = lax.div(p, xs)
        x = lax.rem(lax.rem(p, xs) + ys * xs - y, xs)
        return (y * xs + x) * 2 + c

    chip = lax.div(m, 2)
    row = lax.div(chip, xs)
    q = (xs * row + lax.rem(lax.rem(chip, xs) + row, xs)) * 2 + lax.rem(m, 2)

    def wrap(r):
        return lax.rem(r + 2 * nz, nz)

    def local(src, dst, k):
        return pltpu.make_async_copy(src, dst, loc.at[k])

    locals_ = [
        local(a, av, 0), local(gate, gv, 1), local(up, uv, 2), local(og3, og3v, 3),
        local(b, bv, 4), local(og, ogb.at[m], 5),
        local(w.at[:, pl.ds(0, d_loc)], wb.at[g, 0], 6),
        local(w.at[:, pl.ds(d_loc, d_loc)], wb.at[g, 1], 7),
    ]
    for c in locals_:
        c.start()

    bar = pltpu.get_barrier_semaphore()
    for d in (1, nz - 1):
        pl.semaphore_signal(bar, inc=1, device_id=(wrap(g + d), m), device_id_type=MESH)
    for d in (1, mp - 1):
        pl.semaphore_signal(
            bar, inc=1, device_id=(g, ring_to_mp(lax.rem(q + d, mp))), device_id_type=MESH
        )
    pl.semaphore_wait(bar, 4)

    known = nz // 2 - 1

    def token(d):
        pl.semaphore_signal(
            tok.at[d], inc=1, device_id=(wrap(g + (1 if d == 0 else -1)), m), device_id_type=MESH
        )

    def pass_tokens():
        for d in (0, 1):
            pl.semaphore_wait(tok.at[d], 1)
            token(d)

    class Ring:
        def __init__(self, n, pos, sign, counts, peer, first, buf, ssem, rsem):
            self.n, self.pos, self.sign, self.counts = n, pos, sign, counts
            self.peer, self.first, self.buf, self.ssem, self.rsem = peer, first, buf, ssem, rsem
            self.size = max(max(c) for c in counts)

        def at(self, d, s):
            step = self.sign * s if d == 0 else -self.sign * s
            return lax.rem(self.pos + 2 * self.n - step, self.n)

        def copy(self, d, h, s, src=None):
            dst = self.buf(self.at(d, s), h)
            return pltpu.make_async_remote_copy(
                src_ref=dst if src is None else src,
                dst_ref=dst,
                send_sem=self.ssem.at[d, h, s],
                recv_sem=self.rsem.at[d, h, s],
                device_id=self.peer(self.at(d, -1)),
                device_id_type=MESH,
            )

        def begin(self):
            for h in (0, 1):
                for d in (0, 1):
                    if self.counts[d][h] > 0:
                        self.copy(d, h, 0, self.first(h)).start()

        def arrived(self, d, h, s):
            ref = self.buf(self.at(d, s + 1), h)
            pltpu.make_async_remote_copy(
                src_ref=ref,
                dst_ref=ref,
                send_sem=self.ssem.at[d, h, s],
                recv_sem=self.rsem.at[d, h, s],
                device_id=self.peer(self.pos),
                device_id_type=MESH,
            ).wait_recv()

        def relay(self, s, k=None):
            k = s if k is None else k
            for h in (0, 1):
                for d in (0, 1):
                    if k - 1 < self.counts[d][h]:
                        self.arrived(d, h, s - 1)
                    if k < self.counts[d][h]:
                        self.copy(d, h, s).start()

        def sent(self):
            for h in (0, 1):
                for d in (0, 1):
                    each(
                        0, self.counts[d][h],
                        lambda s, d=d, h=h: self.copy(d, h, s).wait_send(),
                    )

    def halves(n):
        return ((n // 2, n // 2 - 1), (n // 2 - 1, n // 2))

    plane = Ring(
        mp, q, 1, halves(mp), lambda r: (g, ring_to_mp(r)),
        lambda h: og.at[pl.ds(h * half_rows, half_rows), :],
        lambda r, h: ogb.at[ring_to_mp(r), pl.ds(h * half_rows, half_rows), :],
        og_s, og_r,
    )
    wring = Ring(
        nz, g, 1, halves(nz), lambda r: (r, m),
        lambda h: w.at[:, pl.ds(h * d_loc, d_loc)],
        lambda r, h: wb.at[r, h],
        w_s, w_r,
    )

    def some_a(r, h):
        return ab.at[pl.ds(r * own + h * (own // 2), own // 2)]

    aring = Ring(
        nz, g, sign, tuple((r, r) for r in reach), lambda r: (r, m),
        lambda h: apk.at[pl.ds(h * (own // 2), own // 2)], some_a, a_s, a_r,
    )

    wring.begin()
    plane.begin()
    for d in (0, 1):
        token(d)

    lane = lax.broadcasted_iota(jnp.int32, (fh, 128), 1)
    lane64 = lax.broadcasted_iota(jnp.int32, (RANK, 128), 1)

    locals_[0].wait()
    eye = (
        lax.broadcasted_iota(jnp.int32, (RANK, 128), 0) == lane64
    ).astype(F32).astype(BF16)
    for l in range(own):
        t = dot(av[l], eye, 0, 0)
        t = jnp.where(lane < 64, t[:fh], swap(t[fh:])).astype(BF16)
        apk[l] = t
        ab[g * own + l] = t
    aring.begin()

    slots = [soa[aob[g * nblk + k]] for k in range(nblk)]
    owners = [lax.div(s, own) for s in slots]

    def block_for(o):
        at, hit = jnp.int32(0), jnp.int32(0)
        for k in range(nblk):
            e = same(owners[k], o)
            at, hit = at + k * e, hit + e
        blk_of[o] = jnp.minimum(at, nblk - 1)
        hit_of[o] = hit.astype(F32)

    each(0, nz, block_for)

    locals_[1].wait()
    locals_[2].wait()

    def tile_of(j):
        c = pl.ds(pl.multiple_of(j * 128, 128), 128)
        gf = gv[:, c].astype(F32)
        h = gf * jax.nn.sigmoid(gf) * uv[:, c].astype(F32)
        hp[2 * j] = jnp.where(lane < 64, h[:fh], swap(h[fh:])).astype(BF16)
        hp[2 * j + 1] = jnp.where(lane < 64, swap(h[:fh]), h[fh:]).astype(BF16)

    both = min(known - 1, nblk // 2)

    def tile_and_token(j):
        tile_of(j)
        pass_tokens()

    each(0, both, tile_and_token)
    each(both, nblk // 2, tile_of)
    locals_[3].wait()

    def fill(o):
        at, hit = blk_of[o], hit_of[o]
        hs[o, :fh] = (hp[at].astype(F32) * hit).astype(BF16)
        x = (og3v[at].astype(F32) * hit).astype(BF16)
        for k in range(d_loc // 128):
            hs[o, fh + k * 64 : fh + (k + 1) * 64] = x[:, k * 128 : (k + 1) * 128]

    each(0, nz, fill)
    each(both, known - 1, lambda j: pass_tokens())
    for d in (0, 1):
        pl.semaphore_wait(tok.at[d], 1)

    def remote(src, dst, ssem, rsem, z, p):
        return pltpu.make_async_remote_copy(
            src_ref=src, dst_ref=dst, send_sem=ssem, recv_sem=rsem,
            device_id=(z, p), device_id_type=MESH,
        )

    far = wrap(g + nz // 2)

    def piece(ref, i):
        return ref.at[pl.ds(i * mid, mid)]

    def leg1(i):
        to = wrap(g + (quarter if i == 0 else -quarter))
        return remote(piece(hs.at[far], i), xb.at[i], xb_s.at[0, i], xb_r.at[0, i], to, m)

    def leg2(i):
        d = quarter if i == 0 else -quarter
        dst = piece(hr.at[wrap(g - d)], i)
        return remote(xb.at[i], dst, xb_s.at[1, i], xb_r.at[1, i], wrap(g + d), m)

    def leg2_in(i):
        ref = piece(hr.at[far], i)
        return remote(ref, ref, xb_s.at[1, i], xb_r.at[1, i], g, m)

    def block_copy(d):
        to = wrap(g + d)
        return remote(hs.at[to], hr.at[g], x_s.at[d], x_r.at[d], to, m)

    def block_in(d):
        ref = hr.at[wrap(g - d)]
        remote(ref, ref, x_s.at[d], x_r.at[d], g, m).wait_recv()

    def others(body):
        each(1, nz // 2, body)
        each(nz // 2 + 1, nz, body)

    for i in (0, 1):
        leg1(i).start()
    others(lambda d: block_copy(d).start())
    own_hs = local(hs.at[g], hr.at[g], 8)
    own_hs.start()

    def group_tables(j):
        hit, at = jnp.int32(0), jnp.int32(0)
        for k in range(nblk):
            s = soa[aob[j * nblk + k]]
            e = same(lax.div(s, own), g)
            hit, at = hit + e, at + e * lax.rem(s, own)
        slot_in[j] = jnp.minimum(at, own - 1)
        for l in range(own):
            mask_in[j * own + l] = (hit * same(at, l)).astype(F32)

    each(0, nz, group_tables)
    for k in range(nblk):
        o = owners[k]
        dist = lax.rem(sign * (g - o) + nz, nz)
        picked = jnp.minimum(jnp.maximum(dist - reach[0], 0), 1) * jnp.minimum(
            jnp.maximum(nz - reach[1] - dist, 0), 1
        )
        a_at[k] = picked * (g * own) + (1 - picked) * slots[k]
        sel_at[k] = picked * o + (1 - picked) * wrap(g - sign * (reach[0] + 1))
        sel_of[k] = picked.astype(F32)
        quad_of[k] = lax.div(o, 4)
        half_of[k] = lax.rem(lax.div(o, 2), 2).astype(F32)
        odd_of[k] = lax.rem(o, 2).astype(F32)

    each(1, plane.size - 1, lambda s: plane.relay(s, 1))
    plane.relay(plane.size - 1)
    plane.relay(plane.size)
    for c in locals_[4:]:
        c.wait()

    def grad_tile(j, k):
        return hr[j, fh + k * 64 : fh + (k + 1) * 64]

    def rows_of(ref, p):
        return ref.at[pl.ds(units * lax.div(p, 8), units), lax.rem(p, 8)]

    def part_copy(d):
        to = lax.rem(m + d, mp)
        return remote(rows_of(part, to), rsb.at[m], rs_s.at[d], rs_r.at[d], g, to)

    def part_in(d):
        ref = rsb.at[lax.rem(m + mp - d, mp)]
        remote(ref, ref, rs_s.at[d], rs_r.at[d], g, m).wait_recv()

    def fac_copy(d):
        to = lax.rem(m + d, mp)
        return remote(rows_of(fac, m), rows_of(fac, m), fg_s.at[d], fg_r.at[d], g, to)

    def fac_in(d):
        ref = rows_of(fac, lax.rem(m + mp - d, mp))
        remote(ref, ref, fg_s.at[d], fg_r.at[d], g, m).wait_recv()

    my_units = units * lax.div(m, 8)
    my_row = lax.rem(m, 8)

    def stage_partial():
        own_hs.wait()
        others(block_in)
        for i in (0, 1):
            leg2_in(i).wait_recv()

        def one(j):
            l = slot_in[j]
            z = dot(apk[l], hr[j, :fh], 0, 0)
            down = z[:64] + swap(z[64:])
            back = jnp.zeros((RANK, BLK), F32)
            for k in range(d_loc // 128):
                back += dot(bv[l, :, k * 128 : (k + 1) * 128], grad_tile(j, k), 1, 1)
            both = jnp.concatenate([down[:, :64], back], axis=1)
            part[j] = both.reshape(8, 8, 128)

        each(0, nz, one)
        each(1, mp, lambda d: part_copy(d).start())

    def stage_sum():
        rsb[m] = part[pl.ds(my_units, units), my_row]
        each(1, mp, part_in)
        total = lax.fori_loop(
            0, mp, lambda c, t: t + rsb[c], jnp.zeros((units, 8, 128), F32)
        )
        left = lax.broadcasted_iota(jnp.int32, (units, 8, 128), 2) < 64
        total = jnp.where(left, total, 2.0 * total).astype(BF16).astype(F32)
        fac[pl.ds(my_units, units), my_row] = total
        each(1, mp, lambda d: fac_copy(d).start())

    def back_copy(i):
        to = my_units + i
        return remote(fac.at[to, my_row], bk1.at[g], bk_s.at[i], bk_r.at[g], to, m)

    def back_in(o):
        remote(bk1.at[o], bk1.at[o], bk_s.at[0], bk_r.at[o], g, m).wait_recv()

    def stage_back():
        each(1, mp, fac_in)
        for i in range(units):
            @pl.when(my_units + i == g)
            def _():
                bk1[g] = fac[g, my_row]

            @pl.when(my_units + i != g)
            def _():
                back_copy(i).start()

    team = lax.div(g, units)

    def share_copy(d):
        to = lax.rem(m + d, mp)
        return remote(shs, bk2.at[:, my_row], bc_s.at[d], bc_r.at[my_row], g, to)

    def stage_share():
        @pl.when(lax.div(m, 8) == team)
        def _():
            each(1, nz, lambda d: back_in(wrap(g + d)))
            for i in range(nz // 4):
                pairs = [
                    jnp.where(lane64[:8] < 64, swap(bk1[4 * i + 2 * h]), bk1[4 * i + 2 * h + 1])
                    for h in (0, 1)
                ]
                x = jnp.concatenate(pairs, axis=0).astype(BF16)
                shs[i] = x
                bk2[i, my_row] = x
            each(1, mp, lambda d: share_copy(d).start())

    def stage_grads():
        gap[...] = jnp.zeros_like(gap)
        gb[...] = jnp.zeros_like(gb)

        def one(j):
            f = fac[j].reshape(RANK, 128)
            top = jnp.where(lane64 < 64, swap(f), 0.0).astype(BF16)
            bot = jnp.where(lane64 < 64, 0.0, f).astype(BF16)
            pa = dot(jnp.concatenate([top, bot], axis=0), hr[j, :fh], 1, 1)
            pa = pa.astype(BF16).astype(F32)
            down = f.astype(BF16)[:, :64]
            for k in range(d_loc // 128):
                c = slice(k * 128, (k + 1) * 128)
                pb = (2.0 * dot(down, grad_tile(j, k), 1, 0)).astype(BF16).astype(F32)
                for l in range(own):
                    gb[l, :, c] += pb * mask_in[j * own + l]
            for l in range(own):
                gap[l] += pa * mask_in[j * own + l]

        each(0, nz, one)
        for l in range(own):
            ga[l] = jnp.concatenate([gap[l, :64], gap[l, 64:]], axis=1)

    def picks():
        return ((0, wrap(g - sign * reach[0]), sign), (1, wrap(g + sign * reach[1]), -sign))

    def pick_copy(d, o, step, k):
        to = wrap(g + step * k)
        return remote(
            asend.at[d * 3 + k - 1], asel.at[o], sl_s.at[d, k - 1], sl_r.at[d, k - 1], to, m
        )

    def pick_send():
        for d, o, step in picks():
            for k in range(1, tail + 1):
                to = wrap(g + step * k)
                at = jnp.int32(0)
                for i in range(nblk):
                    s = soa[aob[to * nblk + i]]
                    at = at + same(lax.div(s, own), o) * lax.rem(s, own)
                asend[d * 3 + k - 1] = ab[o * own + jnp.minimum(at, own - 1)]
        for d, o, step in picks():
            for k in range(1, tail + 1):
                pick_copy(d, o, step, k).start()

    def pick_in():
        for k in range(1, tail + 1):
            for d, o in ((0, wrap(g - sign * (reach[0] + k))), (1, wrap(g + sign * (reach[1] + k)))):
                ref = asel.at[o]
                remote(ref, ref, sl_s.at[d, k - 1], sl_r.at[d, k - 1], g, m).wait_recv()

    def stage_side():
        pick_in()

        def row_in(t):
            ref = bk2.at[:, t]

            @pl.when(units_first + t != m)
            def _():
                remote(ref, ref, bc_s.at[0], bc_r.at[t], g, m).wait_recv()

        units_first = 8 * team

        each(0, 8, row_in)

        def first_of(k):
            near, sel = ab[a_at[k]].astype(F32), asel[sel_at[k]].astype(F32)
            return near * (1.0 - sel_of[k]) + sel * sel_of[k]

        def back_of(k, side):
            x = bk2[quad_of[k]].astype(F32)
            x = x[:, :8] * (1.0 - half_of[k]) + x[:, 8:] * half_of[k]
            x = x.reshape(RANK, 128)
            keep = odd_of[k] if side else 1.0 - odd_of[k]
            return x * keep + swap(x) * (1.0 - keep)

        def one(j):
            a1, a2 = first_of(2 * j), first_of(2 * j + 1)
            top = jnp.where(lane < 64, a1, swap(a2)).astype(BF16)
            bot = jnp.where(lane < 64, swap(a1), a2).astype(BF16)
            r = jnp.concatenate(
                [
                    jnp.where(lane64 < 64, back_of(2 * j, 0), 0.0),
                    jnp.where(lane64 < 64, 0.0, back_of(2 * j + 1, 1)),
                ],
                axis=0,
            ).astype(BF16)
            c = pl.ds(pl.multiple_of(j * 128, 128), 128)
            out[:fh, c] += dot(top, r, 1, 0)
            out[fh:, c] += dot(bot, r, 1, 0)

        each(0, nblk // 2, one)

    tile = 256 if rows % 256 == 0 else 128

    def multiply(z, h, fresh=False):
        x = wb[z, h]
        for t in range(rows // tile):
            c = slice(t * tile, (t + 1) * tile)
            y = dot(x, ogb[2 * z + h, c, :], 1, 1)
            if fresh:
                out[:, c] = y
            else:
                out[:, c] += y

    def multiply_step(s):
        def one(c):
            d, h = lax.div(c, 2), lax.rem(c, 2)
            multiply(wrap(g + (2 * d - 1) * s), h)

        each(0, 4, one)

    def stage_legs():
        for i in (0, 1):
            remote(xb.at[i], xb.at[i], xb_s.at[0, i], xb_r.at[0, i], g, m).wait_recv()
            leg2(i).start()

    stages = [stage_legs, stage_partial, stage_sum, stage_back, stage_share, stage_grads, stage_side]
    a_steps = [functools.partial(aring.relay, s) for s in range(1, reach[0] + 1)] + [pick_send]
    for s in range(1, nz // 2):
        if a_steps:
            a_steps.pop(0)()
        wring.relay(s)
        if a_steps:
            a_steps.pop(0)()
        if s == 1:
            multiply(g, 0, True)
            multiply(g, 1)
        multiply_step(s)
        if stages and (len(stages) > 1 or not a_steps):
            stages.pop(0)()
    for f in a_steps + stages:
        f()
    wring.relay(nz // 2)
    each(0, 2, lambda c: multiply(far, c))

    plane.sent()
    wring.sent()
    aring.sent()
    others(lambda d: block_copy(d).wait_send())
    for i in (0, 1):
        leg1(i).wait_send()
        leg2(i).wait_send()
    each(1, mp, lambda d: part_copy(d).wait_send())
    each(1, mp, lambda d: fac_copy(d).wait_send())
    for i in range(units):
        @pl.when(my_units + i != g)
        def _():
            back_copy(i).wait_send()

    @pl.when(lax.div(m, 8) == team)
    def _():
        each(1, mp, lambda d: share_copy(d).wait_send())

    for d, o, step in picks():
        for k in range(1, tail + 1):
            pick_copy(d, o, step, k).wait_send()


def shards(og, gate, up, w, a, b, aob, soa):
    nz, mp = lax.axis_size("dp"), lax.axis_size("mp")
    rows, d_loc = og.shape
    ff = gate.shape[1]
    own = a.shape[0]
    nblk = rows // BLK
    fh = ff // 2
    send = fh + d_loc // 2
    units = nz * 8 // mp
    gate, up = gate.T, up.T
    vm = pl.BlockSpec(memory_space=pltpu.VMEM)
    sm = pl.BlockSpec(memory_space=pltpu.SMEM)
    hbm = pl.BlockSpec(memory_space=pl.ANY)
    dma = pltpu.SemaphoreType.DMA
    d_hidden, ga, gb = pl.pallas_call(
        functools.partial(kernel, nz, mp),
        out_shape=(
            jax.ShapeDtypeStruct((ff, rows), F32),
            jax.ShapeDtypeStruct((own, RANK, ff), F32),
            jax.ShapeDtypeStruct((own, RANK, d_loc), F32),
        ),
        in_specs=[sm] * 2 + [hbm] * 7,
        out_specs=(vm,) * 3,
        scratch_shapes=[
            pltpu.VMEM((mp, rows, d_loc), BF16),
            pltpu.VMEM((nz, 2, ff, d_loc), BF16),
            pltpu.VMEM((nz * own, fh, 128), BF16),
            pltpu.VMEM((nz, fh, 128), BF16),
            pltpu.VMEM((own, fh, 128), BF16),
            pltpu.VMEM((6, fh, 128), BF16),
            pltpu.VMEM((nblk, BLK, d_loc), BF16),
            pltpu.VMEM((ff, rows), BF16),
            pltpu.VMEM((ff, rows), BF16),
            pltpu.VMEM((own, RANK, ff), BF16),
            pltpu.VMEM((own, RANK, d_loc), BF16),
            pltpu.VMEM((nblk, fh, 128), BF16),
            pltpu.VMEM((nz, send, 128), BF16),
            pltpu.VMEM((nz, send, 128), BF16),
            pltpu.VMEM((2, send // 2, 128), BF16),
            pltpu.VMEM((nz, 8, 8, 128), F32),
            pltpu.VMEM((mp, units, 8, 128), F32),
            pltpu.VMEM((nz, 8, 8, 128), F32),
            pltpu.VMEM((nz, 8, 128), F32),
            pltpu.VMEM((nz // 4, 16, 128), BF16),
            pltpu.VMEM((nz // 4, 8, 16, 128), BF16),
            pltpu.VMEM((own, 2 * RANK, fh), F32),
            pltpu.SMEM((nz,), jnp.int32),
            pltpu.SMEM((nz,), F32),
            pltpu.SMEM((nz,), jnp.int32),
            pltpu.SMEM((nz * own,), F32),
            pltpu.SMEM((nblk,), jnp.int32),
            pltpu.SMEM((nblk,), jnp.int32),
            pltpu.SMEM((nblk,), F32),
            pltpu.SMEM((nblk,), jnp.int32),
            pltpu.SMEM((nblk,), F32),
            pltpu.SMEM((nblk,), F32),
            dma((2, 2, mp // 2)), dma((2, 2, mp // 2)),
            dma((2, 2, nz // 2)), dma((2, 2, nz // 2)),
            dma((2, 2, nz // 2)), dma((2, 2, nz // 2)),
            dma((nz,)), dma((nz,)),
            dma((mp,)), dma((mp,)),
            dma((mp,)), dma((mp,)),
            dma((units,)), dma((nz,)),
            dma((mp,)), dma((8,)),
            dma((2, 3)), dma((2, 3)),
            dma((2, 2)), dma((2, 2)),
            dma((9,)),
            pltpu.SemaphoreType.REGULAR((2,)),
        ],
        compiler_params=pltpu.CompilerParams(
            collective_id=0, has_side_effects=True, vmem_limit_bytes=67_000_000
        ),
    )(aob, soa, og, og.reshape(nblk, BLK, d_loc), gate, up, w, a, b)
    gf, uf = gate.astype(F32), up.astype(F32)
    s = jax.nn.sigmoid(gf)
    d_gate = (d_hidden * uf * s * (1.0 + gf * (1.0 - s))).astype(BF16)
    d_up = (d_hidden * (gf * s)).astype(BF16)
    return d_gate.T, d_up.T, ga, gb


def solution(mesh):
    in_specs = (
        P("dp", "mp"),
        P("dp", "mp"),
        P("dp", "mp"),
        P("mp", "dp"),
        P("dp", None, "mp"),
        P("dp", None, "mp"),
        P(),
        P(),
    )
    out_specs = (P("dp", "mp"), P("dp", "mp"), P("dp", None, "mp"), P("dp", None, "mp"))
    return jax.shard_map(shards, mesh=mesh, in_specs=in_specs, out_specs=out_specs, check_vma=False)
```

```python
import functools
import math

import jax
import jax.numpy as jnp
from jax import lax
from jax.experimental import pallas as pl
from jax.experimental.pallas import tpu as pltpu
from jax.sharding import PartitionSpec as P

BLK = 64
RANK = 64
MESH = pl.DeviceIdType.MESH
F32 = jnp.float32
BF16 = jnp.bfloat16


def dot(x, y, cx, cy):
    return lax.dot_general(x, y, (((cx,), (cy,)), ((), ())), preferred_element_type=F32)


def each(lo, hi, body):
    def step(i, carry):
        body(i)
        return carry

    if hi > lo:
        lax.fori_loop(lo, hi, step, 0)


def same(x, y):
    return 1 - jnp.minimum(jnp.abs(x - y), 1)


def swap(x):
    return pltpu.roll(x, 64, 1)


def kernel(
    nz, mp,
    aob, soa, og, og3, gate, up, w, a, b,
    out, ga, gb,
    ogb, wb, ab, asel, apk, asend, og3v, gv, uv, av, bv, hp, hs, hr, xb, part, rsb, fac, bk1, shs, bk2, gap,
    blk_of, hit_of, slot_in, mask_in, a_at, sel_at, sel_of, quad_of, half_of, odd_of,
    og_s, og_r, w_s, w_r, a_s, a_r, x_s, x_r, rs_s, rs_r, fg_s, fg_r, bk_s, bk_r, bc_s, bc_r,
    sl_s, sl_r, xb_s, xb_r, loc, tok,
):
    xs = math.isqrt(mp // 2)
    ys = mp // 2 // xs
    rows, d_loc = og.shape
    ff = gate.shape[0]
    nblk = rows // BLK
    own = a.shape[0]
    half_rows = rows // 2
    fh = ff // 2
    units = nz * 8 // mp
    tail = min(3, nz // 2 - 1)
    reach = (nz // 2 - tail, nz // 2 - 1 - tail)
    quarter = nz // 4
    mid = (fh + d_loc // 2) // 2
    g = lax.axis_index("dp")
    m = lax.axis_index("mp")
    sign = 1 - 2 * lax.rem(m, 2)

    def ring_to_mp(q):
        p, c = lax.div(q, 2), lax.rem(q, 2)
        y = lax.div(p, xs)
        x = lax.rem(lax.rem(p, xs) + ys * xs - y, xs)
        return (y * xs + x) * 2 + c

    chip = lax.div(m, 2)
    row = lax.div(chip, xs)
    q = (xs * row + lax.rem(lax.rem(chip, xs) + row, xs)) * 2 + lax.rem(m, 2)

    def wrap(r):
        return lax.rem(r + 2 * nz, nz)

    def local(src, dst, k):
        return pltpu.make_async_copy(src, dst, loc.at[k])

    locals_ = [
        local(a, av, 0), local(gate, gv, 1), local(up, uv, 2), local(og3, og3v, 3),
        local(b, bv, 4), local(og, ogb.at[m], 5),
        local(w.at[:, pl.ds(0, d_loc)], wb.at[g, 0], 6),
        local(w.at[:, pl.ds(d_loc, d_loc)], wb.at[g, 1], 7),
    ]
    for c in locals_:
        c.start()

    bar = pltpu.get_barrier_semaphore()
    for d in (1, nz - 1):
        pl.semaphore_signal(bar, inc=1, device_id=(wrap(g + d), m), device_id_type=MESH)
    for d in (1, mp - 1):
        pl.semaphore_signal(
            bar, inc=1, device_id=(g, ring_to_mp(lax.rem(q + d, mp))), device_id_type=MESH
        )
    pl.semaphore_wait(bar, 4)

    known = nz // 2 - 1

    def token(d):
        pl.semaphore_signal(
            tok.at[d], inc=1, device_id=(wrap(g + (1 if d == 0 else -1)), m), device_id_type=MESH
        )

    def pass_tokens():
        for d in (0, 1):
            pl.semaphore_wait(tok.at[d], 1)
            token(d)

    class Ring:
        def __init__(self, n, pos, sign, counts, peer, first, buf, ssem, rsem):
            self.n, self.pos, self.sign, self.counts = n, pos, sign, counts
            self.peer, self.first, self.buf, self.ssem, self.rsem = peer, first, buf, ssem, rsem
            self.size = max(max(c) for c in counts)

        def at(self, d, s):
            step = self.sign * s if d == 0 else -self.sign * s
            return lax.rem(self.pos + 2 * self.n - step, self.n)

        def copy(self, d, h, s, src=None):
            dst = self.buf(self.at(d, s), h)
            return pltpu.make_async_remote_copy(
                src_ref=dst if src is None else src,
                dst_ref=dst,
                send_sem=self.ssem.at[d, h, s],
                recv_sem=self.rsem.at[d, h, s],
                device_id=self.peer(self.at(d, -1)),
                device_id_type=MESH,
            )

        def begin(self):
            for h in (0, 1):
                for d in (0, 1):
                    if self.counts[d][h] > 0:
                        self.copy(d, h, 0, self.first(h)).start()

        def arrived(self, d, h, s):
            ref = self.buf(self.at(d, s + 1), h)
            pltpu.make_async_remote_copy(
                src_ref=ref,
                dst_ref=ref,
                send_sem=self.ssem.at[d, h, s],
                recv_sem=self.rsem.at[d, h, s],
                device_id=self.peer(self.pos),
                device_id_type=MESH,
            ).wait_recv()

        def relay(self, s, k=None):
            k = s if k is None else k
            for h in (0, 1):
                for d in (0, 1):
                    if k - 1 < self.counts[d][h]:
                        self.arrived(d, h, s - 1)
                    if k < self.counts[d][h]:
                        self.copy(d, h, s).start()

        def sent(self):
            for h in (0, 1):
                for d in (0, 1):
                    each(
                        0, self.counts[d][h],
                        lambda s, d=d, h=h: self.copy(d, h, s).wait_send(),
                    )

    def halves(n):
        return ((n // 2, n // 2 - 1), (n // 2 - 1, n // 2))

    plane = Ring(
        mp, q, 1, halves(mp), lambda r: (g, ring_to_mp(r)),
        lambda h: og.at[pl.ds(h * half_rows, half_rows), :],
        lambda r, h: ogb.at[ring_to_mp(r), pl.ds(h * half_rows, half_rows), :],
        og_s, og_r,
    )
    wring = Ring(
        nz, g, 1, halves(nz), lambda r: (r, m),
        lambda h: w.at[:, pl.ds(h * d_loc, d_loc)],
        lambda r, h: wb.at[r, h],
        w_s, w_r,
    )

    def some_a(r, h):
        return ab.at[pl.ds(r * own + h * (own // 2), own // 2)]

    aring = Ring(
        nz, g, sign, tuple((r, r) for r in reach), lambda r: (r, m),
        lambda h: apk.at[pl.ds(h * (own // 2), own // 2)], some_a, a_s, a_r,
    )

    wring.begin()
    plane.begin()
    for d in (0, 1):
        token(d)

    lane = lax.broadcasted_iota(jnp.int32, (fh, 128), 1)
    lane64 = lax.broadcasted_iota(jnp.int32, (RANK, 128), 1)

    locals_[0].wait()
    eye = (
        lax.broadcasted_iota(jnp.int32, (RANK, 128), 0) == lane64
    ).astype(F32).astype(BF16)
    for l in range(own):
        t = dot(av[l], eye, 0, 0)
        t = jnp.where(lane < 64, t[:fh], swap(t[fh:])).astype(BF16)
        apk[l] = t
        ab[g * own + l] = t
    aring.begin()

    slots = [soa[aob[g * nblk + k]] for k in range(nblk)]
    owners = [lax.div(s, own) for s in slots]

    def block_for(o):
        at, hit = jnp.int32(0), jnp.int32(0)
        for k in range(nblk):
            e = same(owners[k], o)
            at, hit = at + k * e, hit + e
        blk_of[o] = jnp.minimum(at, nblk - 1)
        hit_of[o] = hit.astype(F32)

    each(0, nz, block_for)

    locals_[1].wait()
    locals_[2].wait()

    def tile_of(j):
        c = pl.ds(pl.multiple_of(j * 128, 128), 128)
        gf = gv[:, c].astype(F32)
        h = gf * jax.nn.sigmoid(gf) * uv[:, c].astype(F32)
        hp[2 * j] = jnp.where(lane < 64, h[:fh], swap(h[fh:])).astype(BF16)
        hp[2 * j + 1] = jnp.where(lane < 64, swap(h[:fh]), h[fh:]).astype(BF16)

    both = min(known - 1, nblk // 2)

    def tile_and_token(j):
        tile_of(j)
        pass_tokens()

    each(0, both, tile_and_token)
    each(both, nblk // 2, tile_of)
    locals_[3].wait()

    def fill(o):
        at, hit = blk_of[o], hit_of[o]
        hs[o, :fh] = (hp[at].astype(F32) * hit).astype(BF16)
        x = (og3v[at].astype(F32) * hit).astype(BF16)
        for k in range(d_loc // 128):
            hs[o, fh + k * 64 : fh + (k + 1) * 64] = x[:, k * 128 : (k + 1) * 128]

    each(0, nz, fill)
    each(both, known - 1, lambda j: pass_tokens())
    for d in (0, 1):
        pl.semaphore_wait(tok.at[d], 1)

    def remote(src, dst, ssem, rsem, z, p):
        return pltpu.make_async_remote_copy(
            src_ref=src, dst_ref=dst, send_sem=ssem, recv_sem=rsem,
            device_id=(z, p), device_id_type=MESH,
        )

    far = wrap(g + nz // 2)

    def piece(ref, i):
        return ref.at[pl.ds(i * mid, mid)]

    def leg1(i):
        to = wrap(g + (quarter if i == 0 else -quarter))
        return remote(piece(hs.at[far], i), xb.at[i], xb_s.at[0, i], xb_r.at[0, i], to, m)

    def leg2(i):
        d = quarter if i == 0 else -quarter
        dst = piece(hr.at[wrap(g - d)], i)
        return remote(xb.at[i], dst, xb_s.at[1, i], xb_r.at[1, i], wrap(g + d), m)

    def leg2_in(i):
        ref = piece(hr.at[far], i)
        return remote(ref, ref, xb_s.at[1, i], xb_r.at[1, i], g, m)

    def block_copy(d):
        to = wrap(g + d)
        return remote(hs.at[to], hr.at[g], x_s.at[d], x_r.at[d], to, m)

    def block_in(d):
        ref = hr.at[wrap(g - d)]
        remote(ref, ref, x_s.at[d], x_r.at[d], g, m).wait_recv()

    def others(body):
        each(1, nz // 2, body)
        each(nz // 2 + 1, nz, body)

    for i in (0, 1):
        leg1(i).start()
    others(lambda d: block_copy(d).start())
    own_hs = local(hs.at[g], hr.at[g], 8)
    own_hs.start()

    def group_tables(j):
        hit, at = jnp.int32(0), jnp.int32(0)
        for k in range(nblk):
            s = soa[aob[j * nblk + k]]
            e = same(lax.div(s, own), g)
            hit, at = hit + e, at + e * lax.rem(s, own)
        slot_in[j] = jnp.minimum(at, own - 1)
        for l in range(own):
            mask_in[j * own + l] = (hit * same(at, l)).astype(F32)

    each(0, nz, group_tables)
    for k in range(nblk):
        o = owners[k]
        dist = lax.rem(sign * (g - o) + nz, nz)
        picked = jnp.minimum(jnp.maximum(dist - reach[0], 0), 1) * jnp.minimum(
            jnp.maximum(nz - reach[1] - dist, 0), 1
        )
        a_at[k] = picked * (g * own) + (1 - picked) * slots[k]
        sel_at[k] = picked * o + (1 - picked) * wrap(g - sign * (reach[0] + 1))
        sel_of[k] = picked.astype(F32)
        quad_of[k] = lax.div(o, 4)
        half_of[k] = lax.rem(lax.div(o, 2), 2).astype(F32)
        odd_of[k] = lax.rem(o, 2).astype(F32)

    cut = plane.size // 2
    each(1, cut, lambda s: plane.relay(s, 1))
    wring.relay(1)
    each(cut, plane.size - 1, lambda s: plane.relay(s, 1))
    plane.relay(plane.size - 1)
    plane.relay(plane.size)
    for c in locals_[4:]:
        c.wait()

    def grad_tile(j, k):
        return hr[j, fh + k * 64 : fh + (k + 1) * 64]

    def rows_of(ref, p):
        return ref.at[pl.ds(units * lax.div(p, 8), units), lax.rem(p, 8)]

    def part_copy(d):
        to = lax.rem(m + d, mp)
        return remote(rows_of(part, to), rsb.at[m], rs_s.at[d], rs_r.at[d], g, to)

    def part_in(d):
        ref = rsb.at[lax.rem(m + mp - d, mp)]
        remote(ref, ref, rs_s.at[d], rs_r.at[d], g, m).wait_recv()

    def fac_copy(d):
        to = lax.rem(m + d, mp)
        return remote(rows_of(fac, m), rows_of(fac, m), fg_s.at[d], fg_r.at[d], g, to)

    def fac_in(d):
        ref = rows_of(fac, lax.rem(m + mp - d, mp))
        remote(ref, ref, fg_s.at[d], fg_r.at[d], g, m).wait_recv()

    my_units = units * lax.div(m, 8)
    my_row = lax.rem(m, 8)

    def stage_partial():
        own_hs.wait()
        others(block_in)
        for i in (0, 1):
            leg2_in(i).wait_recv()

        def one(j):
            l = slot_in[j]
            z = dot(apk[l], hr[j, :fh], 0, 0)
            down = z[:64] + swap(z[64:])
            back = jnp.zeros((RANK, BLK), F32)
            for k in range(d_loc // 128):
                back += dot(bv[l, :, k * 128 : (k + 1) * 128], grad_tile(j, k), 1, 1)
            both = jnp.concatenate([down[:, :64], back], axis=1)
            part[j] = both.reshape(8, 8, 128)

        each(0, nz, one)
        each(1, mp, lambda d: part_copy(d).start())

    def stage_sum():
        rsb[m] = part[pl.ds(my_units, units), my_row]
        each(1, mp, part_in)
        total = lax.fori_loop(
            0, mp, lambda c, t: t + rsb[c], jnp.zeros((units, 8, 128), F32)
        )
        left = lax.broadcasted_iota(jnp.int32, (units, 8, 128), 2) < 64
        total = jnp.where(left, total, 2.0 * total).astype(BF16).astype(F32)
        fac[pl.ds(my_units, units), my_row] = total
        each(1, mp, lambda d: fac_copy(d).start())

    def back_copy(i):
        to = my_units + i
        return remote(fac.at[to, my_row], bk1.at[g], bk_s.at[i], bk_r.at[g], to, m)

    def back_in(o):
        remote(bk1.at[o], bk1.at[o], bk_s.at[0], bk_r.at[o], g, m).wait_recv()

    def stage_back():
        each(1, mp, fac_in)
        for i in range(units):
            @pl.when(my_units + i == g)
            def _():
                bk1[g] = fac[g, my_row]

            @pl.when(my_units + i != g)
            def _():
                back_copy(i).start()

    team = lax.div(g, units)

    def share_copy(d):
        to = lax.rem(m + d, mp)
        return remote(shs, bk2.at[:, my_row], bc_s.at[d], bc_r.at[my_row], g, to)

    def stage_share():
        @pl.when(lax.div(m, 8) == team)
        def _():
            each(1, nz, lambda d: back_in(wrap(g + d)))
            for i in range(nz // 4):
                pairs = [
                    jnp.where(lane64[:8] < 64, swap(bk1[4 * i + 2 * h]), bk1[4 * i + 2 * h + 1])
                    for h in (0, 1)
                ]
                x = jnp.concatenate(pairs, axis=0).astype(BF16)
                shs[i] = x
                bk2[i, my_row] = x
            each(1, mp, lambda d: share_copy(d).start())

    def stage_grads():
        gap[...] = jnp.zeros_like(gap)
        gb[...] = jnp.zeros_like(gb)

        def one(j):
            f = fac[j].reshape(RANK, 128)
            top = jnp.where(lane64 < 64, swap(f), 0.0).astype(BF16)
            bot = jnp.where(lane64 < 64, 0.0, f).astype(BF16)
            pa = dot(jnp.concatenate([top, bot], axis=0), hr[j, :fh], 1, 1)
            pa = pa.astype(BF16).astype(F32)
            down = f.astype(BF16)[:, :64]
            for k in range(d_loc // 128):
                c = slice(k * 128, (k + 1) * 128)
                pb = (2.0 * dot(down, grad_tile(j, k), 1, 0)).astype(BF16).astype(F32)
                for l in range(own):
                    gb[l, :, c] += pb * mask_in[j * own + l]
            for l in range(own):
                gap[l] += pa * mask_in[j * own + l]

        each(0, nz, one)
        for l in range(own):
            ga[l] = jnp.concatenate([gap[l, :64], gap[l, 64:]], axis=1)

    def picks():
        return ((0, wrap(g - sign * reach[0]), sign), (1, wrap(g + sign * reach[1]), -sign))

    def pick_copy(d, o, step, k):
        to = wrap(g + step * k)
        return remote(
            asend.at[d * 3 + k - 1], asel.at[o], sl_s.at[d, k - 1], sl_r.at[d, k - 1], to, m
        )

    def pick_send():
        for d, o, step in picks():
            for k in range(1, tail + 1):
                to = wrap(g + step * k)
                at = jnp.int32(0)
                for i in range(nblk):
                    s = soa[aob[to * nblk + i]]
                    at = at + same(lax.div(s, own), o) * lax.rem(s, own)
                asend[d * 3 + k - 1] = ab[o * own + jnp.minimum(at, own - 1)]
        for d, o, step in picks():
            for k in range(1, tail + 1):
                pick_copy(d, o, step, k).start()

    def pick_in():
        for k in range(1, tail + 1):
            for d, o in ((0, wrap(g - sign * (reach[0] + k))), (1, wrap(g + sign * (reach[1] + k)))):
                ref = asel.at[o]
                remote(ref, ref, sl_s.at[d, k - 1], sl_r.at[d, k - 1], g, m).wait_recv()

    def stage_side():
        pick_in()

        def row_in(t):
            ref = bk2.at[:, t]

            @pl.when(units_first + t != m)
            def _():
                remote(ref, ref, bc_s.at[0], bc_r.at[t], g, m).wait_recv()

        units_first = 8 * team

        each(0, 8, row_in)

        def first_of(k):
            near, sel = ab[a_at[k]].astype(F32), asel[sel_at[k]].astype(F32)
            return near * (1.0 - sel_of[k]) + sel * sel_of[k]

        def back_of(k, side):
            x = bk2[quad_of[k]].astype(F32)
            x = x[:, :8] * (1.0 - half_of[k]) + x[:, 8:] * half_of[k]
            x = x.reshape(RANK, 128)
            keep = odd_of[k] if side else 1.0 - odd_of[k]
            return x * keep + swap(x) * (1.0 - keep)

        def one(j):
            a1, a2 = first_of(2 * j), first_of(2 * j + 1)
            top = jnp.where(lane < 64, a1, swap(a2)).astype(BF16)
            bot = jnp.where(lane < 64, swap(a1), a2).astype(BF16)
            r = jnp.concatenate(
                [
                    jnp.where(lane64 < 64, back_of(2 * j, 0), 0.0),
                    jnp.where(lane64 < 64, 0.0, back_of(2 * j + 1, 1)),
                ],
                axis=0,
            ).astype(BF16)
            c = pl.ds(pl.multiple_of(j * 128, 128), 128)
            out[:fh, c] += dot(top, r, 1, 0)
            out[fh:, c] += dot(bot, r, 1, 0)

        each(0, nblk // 2, one)

    tile = 256 if rows % 256 == 0 else 128

    def multiply(z, h, fresh=False):
        x = wb[z, h]
        for t in range(rows // tile):
            c = slice(t * tile, (t + 1) * tile)
            y = dot(x, ogb[2 * z + h, c, :], 1, 1)
            if fresh:
                out[:, c] = y
            else:
                out[:, c] += y

    def multiply_step(s):
        def one(c):
            d, h = lax.div(c, 2), lax.rem(c, 2)
            multiply(wrap(g + (2 * d - 1) * s), h)

        each(0, 4, one)

    def stage_legs():
        for i in (0, 1):
            remote(xb.at[i], xb.at[i], xb_s.at[0, i], xb_r.at[0, i], g, m).wait_recv()
            leg2(i).start()

    stages = [stage_legs, stage_partial, stage_sum, stage_back, stage_share, stage_grads, stage_side]
    a_steps = [functools.partial(aring.relay, s) for s in range(1, reach[0] + 1)] + [pick_send]
    for s in range(1, nz // 2):
        if a_steps:
            a_steps.pop(0)()
        if s > 1:
            wring.relay(s)
        if s == 1:
            multiply(g, 0, True)
            multiply(g, 1)
        multiply_step(s)
        if stages and (len(stages) > 1 or not a_steps):
            stages.pop(0)()
    for f in a_steps + stages:
        f()
    wring.relay(nz // 2)
    each(0, 2, lambda c: multiply(far, c))

    plane.sent()
    wring.sent()
    aring.sent()
    others(lambda d: block_copy(d).wait_send())
    for i in (0, 1):
        leg1(i).wait_send()
        leg2(i).wait_send()
    each(1, mp, lambda d: part_copy(d).wait_send())
    each(1, mp, lambda d: fac_copy(d).wait_send())
    for i in range(units):
        @pl.when(my_units + i != g)
        def _():
            back_copy(i).wait_send()

    @pl.when(lax.div(m, 8) == team)
    def _():
        each(1, mp, lambda d: share_copy(d).wait_send())

    for d, o, step in picks():
        for k in range(1, tail + 1):
            pick_copy(d, o, step, k).wait_send()


def shards(og, gate, up, w, a, b, aob, soa):
    nz, mp = lax.axis_size("dp"), lax.axis_size("mp")
    rows, d_loc = og.shape
    ff = gate.shape[1]
    own = a.shape[0]
    nblk = rows // BLK
    fh = ff // 2
    send = fh + d_loc // 2
    units = nz * 8 // mp
    gate, up = gate.T, up.T
    vm = pl.BlockSpec(memory_space=pltpu.VMEM)
    sm = pl.BlockSpec(memory_space=pltpu.SMEM)
    hbm = pl.BlockSpec(memory_space=pl.ANY)
    dma = pltpu.SemaphoreType.DMA
    d_hidden, ga, gb = pl.pallas_call(
        functools.partial(kernel, nz, mp),
        out_shape=(
            jax.ShapeDtypeStruct((ff, rows), F32),
            jax.ShapeDtypeStruct((own, RANK, ff), F32),
            jax.ShapeDtypeStruct((own, RANK, d_loc), F32),
        ),
        in_specs=[sm] * 2 + [hbm] * 7,
        out_specs=(vm,) * 3,
        scratch_shapes=[
            pltpu.VMEM((mp, rows, d_loc), BF16),
            pltpu.VMEM((nz, 2, ff, d_loc), BF16),
            pltpu.VMEM((nz * own, fh, 128), BF16),
            pltpu.VMEM((nz, fh, 128), BF16),
            pltpu.VMEM((own, fh, 128), BF16),
            pltpu.VMEM((6, fh, 128), BF16),
            pltpu.VMEM((nblk, BLK, d_loc), BF16),
            pltpu.VMEM((ff, rows), BF16),
            pltpu.VMEM((ff, rows), BF16),
            pltpu.VMEM((own, RANK, ff), BF16),
            pltpu.VMEM((own, RANK, d_loc), BF16),
            pltpu.VMEM((nblk, fh, 128), BF16),
            pltpu.VMEM((nz, send, 128), BF16),
            pltpu.VMEM((nz, send, 128), BF16),
            pltpu.VMEM((2, send // 2, 128), BF16),
            pltpu.VMEM((nz, 8, 8, 128), F32),
            pltpu.VMEM((mp, units, 8, 128), F32),
            pltpu.VMEM((nz, 8, 8, 128), F32),
            pltpu.VMEM((nz, 8, 128), F32),
            pltpu.VMEM((nz // 4, 16, 128), BF16),
            pltpu.VMEM((nz // 4, 8, 16, 128), BF16),
            pltpu.VMEM((own, 2 * RANK, fh), F32),
            pltpu.SMEM((nz,), jnp.int32),
            pltpu.SMEM((nz,), F32),
            pltpu.SMEM((nz,), jnp.int32),
            pltpu.SMEM((nz * own,), F32),
            pltpu.SMEM((nblk,), jnp.int32),
            pltpu.SMEM((nblk,), jnp.int32),
            pltpu.SMEM((nblk,), F32),
            pltpu.SMEM((nblk,), jnp.int32),
            pltpu.SMEM((nblk,), F32),
            pltpu.SMEM((nblk,), F32),
            dma((2, 2, mp // 2)), dma((2, 2, mp // 2)),
            dma((2, 2, nz // 2)), dma((2, 2, nz // 2)),
            dma((2, 2, nz // 2)), dma((2, 2, nz // 2)),
            dma((nz,)), dma((nz,)),
            dma((mp,)), dma((mp,)),
            dma((mp,)), dma((mp,)),
            dma((units,)), dma((nz,)),
            dma((mp,)), dma((8,)),
            dma((2, 3)), dma((2, 3)),
            dma((2, 2)), dma((2, 2)),
            dma((9,)),
            pltpu.SemaphoreType.REGULAR((2,)),
        ],
        compiler_params=pltpu.CompilerParams(
            collective_id=0, has_side_effects=True, vmem_limit_bytes=67_000_000
        ),
    )(aob, soa, og, og.reshape(nblk, BLK, d_loc), gate, up, w, a, b)
    gf, uf = gate.astype(F32), up.astype(F32)
    s = jax.nn.sigmoid(gf)
    d_gate = (d_hidden * uf * s * (1.0 + gf * (1.0 - s))).astype(BF16)
    d_up = (d_hidden * (gf * s)).astype(BF16)
    return d_gate.T, d_up.T, ga, gb


def solution(mesh):
    in_specs = (
        P("dp", "mp"),
        P("dp", "mp"),
        P("dp", "mp"),
        P("mp", "dp"),
        P("dp", None, "mp"),
        P("dp", None, "mp"),
        P(),
        P(),
    )
    out_specs = (P("dp", "mp"), P("dp", "mp"), P("dp", None, "mp"), P("dp", None, "mp"))
    return jax.shard_map(shards, mesh=mesh, in_specs=in_specs, out_specs=out_specs, check_vma=False)
```

```python
import functools
import math

import jax
import jax.numpy as jnp
from jax import lax
from jax.experimental import pallas as pl
from jax.experimental.pallas import tpu as pltpu
from jax.sharding import PartitionSpec as P

BLK = 64
RANK = 64
MESH = pl.DeviceIdType.MESH
F32 = jnp.float32
BF16 = jnp.bfloat16


def dot(x, y, cx, cy):
    return lax.dot_general(x, y, (((cx,), (cy,)), ((), ())), preferred_element_type=F32)


def each(lo, hi, body):
    def step(i, carry):
        body(i)
        return carry

    if hi > lo:
        lax.fori_loop(lo, hi, step, 0)


def same(x, y):
    return 1 - jnp.minimum(jnp.abs(x - y), 1)


def swap(x):
    return pltpu.roll(x, 64, 1)


def kernel(
    nz, mp,
    aob, soa, og, og3, gate, up, w, a, b,
    out, ga_out, gb_out,
    ogb, wb, ab, asel, apk, asend, og3v, gv, uv, av, bv, hp, hs, hr, xb, part, rsb, fac, bk1, shs, bk2, gap, ga, gb,
    blk_of, hit_of, slot_in, mask_in, a_at, sel_at, sel_of, quad_of, half_of, odd_of,
    og_s, og_r, w_s, w_r, a_s, a_r, x_s, x_r, rs_s, rs_r, fg_s, fg_r, bk_s, bk_r, bc_s, bc_r,
    sl_s, sl_r, xb_s, xb_r, loc, tok,
):
    xs = math.isqrt(mp // 2)
    ys = mp // 2 // xs
    rows, d_loc = og.shape
    ff = gate.shape[0]
    nblk = rows // BLK
    own = a.shape[0]
    half_rows = rows // 2
    fh = ff // 2
    units = nz * 8 // mp
    tail = min(3, nz // 2 - 1)
    reach = (nz // 2 - tail, nz // 2 - 1 - tail)
    quarter = nz // 4
    mid = (fh + d_loc // 2) // 2
    g = lax.axis_index("dp")
    m = lax.axis_index("mp")
    sign = 1 - 2 * lax.rem(m, 2)

    def ring_to_mp(q):
        p, c = lax.div(q, 2), lax.rem(q, 2)
        y = lax.div(p, xs)
        x = lax.rem(lax.rem(p, xs) + ys * xs - y, xs)
        return (y * xs + x) * 2 + c

    chip = lax.div(m, 2)
    row = lax.div(chip, xs)
    q = (xs * row + lax.rem(lax.rem(chip, xs) + row, xs)) * 2 + lax.rem(m, 2)

    def wrap(r):
        return lax.rem(r + 2 * nz, nz)

    def local(src, dst, k):
        return pltpu.make_async_copy(src, dst, loc.at[k])

    locals_ = [
        local(a, av, 0), local(gate, gv, 1), local(up, uv, 2), local(og3, og3v, 3),
        local(b, bv, 4), local(og, ogb.at[m], 5),
        local(w.at[:, pl.ds(0, d_loc)], wb.at[g, 0], 6),
        local(w.at[:, pl.ds(d_loc, d_loc)], wb.at[g, 1], 7),
    ]
    for c in locals_:
        c.start()

    bar = pltpu.get_barrier_semaphore()
    for d in (1, nz - 1):
        pl.semaphore_signal(bar, inc=1, device_id=(wrap(g + d), m), device_id_type=MESH)
    for d in (1, mp - 1):
        pl.semaphore_signal(
            bar, inc=1, device_id=(g, ring_to_mp(lax.rem(q + d, mp))), device_id_type=MESH
        )
    pl.semaphore_wait(bar, 4)

    known = nz // 2 - 1

    def token(d):
        pl.semaphore_signal(
            tok.at[d], inc=1, device_id=(wrap(g + (1 if d == 0 else -1)), m), device_id_type=MESH
        )

    def pass_tokens():
        for d in (0, 1):
            pl.semaphore_wait(tok.at[d], 1)
            token(d)

    class Ring:
        def __init__(self, n, pos, sign, counts, peer, first, buf, ssem, rsem):
            self.n, self.pos, self.sign, self.counts = n, pos, sign, counts
            self.peer, self.first, self.buf, self.ssem, self.rsem = peer, first, buf, ssem, rsem
            self.size = max(max(c) for c in counts)

        def at(self, d, s):
            step = self.sign * s if d == 0 else -self.sign * s
            return lax.rem(self.pos + 2 * self.n - step, self.n)

        def copy(self, d, h, s, src=None):
            dst = self.buf(self.at(d, s), h)
            return pltpu.make_async_remote_copy(
                src_ref=dst if src is None else src,
                dst_ref=dst,
                send_sem=self.ssem.at[d, h, s],
                recv_sem=self.rsem.at[d, h, s],
                device_id=self.peer(self.at(d, -1)),
                device_id_type=MESH,
            )

        def begin(self):
            for h in (0, 1):
                for d in (0, 1):
                    if self.counts[d][h] > 0:
                        self.copy(d, h, 0, self.first(h)).start()

        def arrived(self, d, h, s):
            ref = self.buf(self.at(d, s + 1), h)
            pltpu.make_async_remote_copy(
                src_ref=ref,
                dst_ref=ref,
                send_sem=self.ssem.at[d, h, s],
                recv_sem=self.rsem.at[d, h, s],
                device_id=self.peer(self.pos),
                device_id_type=MESH,
            ).wait_recv()

        def relay(self, s, k=None):
            k = s if k is None else k
            for h in (0, 1):
                for d in (0, 1):
                    if k - 1 < self.counts[d][h]:
                        self.arrived(d, h, s - 1)
                    if k < self.counts[d][h]:
                        self.copy(d, h, s).start()

        def sent(self):
            for h in (0, 1):
                for d in (0, 1):
                    each(
                        0, self.counts[d][h],
                        lambda s, d=d, h=h: self.copy(d, h, s).wait_send(),
                    )

    def halves(n):
        return ((n // 2, n // 2 - 1), (n // 2 - 1, n // 2))

    plane = Ring(
        mp, q, 1, halves(mp), lambda r: (g, ring_to_mp(r)),
        lambda h: og.at[pl.ds(h * half_rows, half_rows), :],
        lambda r, h: ogb.at[ring_to_mp(r), pl.ds(h * half_rows, half_rows), :],
        og_s, og_r,
    )
    wring = Ring(
        nz, g, 1, halves(nz), lambda r: (r, m),
        lambda h: w.at[:, pl.ds(h * d_loc, d_loc)],
        lambda r, h: wb.at[r, h],
        w_s, w_r,
    )

    def some_a(r, h):
        return ab.at[pl.ds(r * own + h * (own // 2), own // 2)]

    aring = Ring(
        nz, g, sign, tuple((r, r) for r in reach), lambda r: (r, m),
        lambda h: apk.at[pl.ds(h * (own // 2), own // 2)], some_a, a_s, a_r,
    )

    wring.begin()
    plane.begin()
    for d in (0, 1):
        token(d)

    lane = lax.broadcasted_iota(jnp.int32, (fh, 128), 1)
    lane64 = lax.broadcasted_iota(jnp.int32, (RANK, 128), 1)

    locals_[0].wait()
    eye = (
        lax.broadcasted_iota(jnp.int32, (RANK, 128), 0) == lane64
    ).astype(F32).astype(BF16)
    for l in range(own):
        t = dot(av[l], eye, 0, 0)
        t = jnp.where(lane < 64, t[:fh], swap(t[fh:])).astype(BF16)
        apk[l] = t
        ab[g * own + l] = t
    aring.begin()

    slots = [soa[aob[g * nblk + k]] for k in range(nblk)]
    owners = [lax.div(s, own) for s in slots]

    def block_for(o):
        at, hit = jnp.int32(0), jnp.int32(0)
        for k in range(nblk):
            e = same(owners[k], o)
            at, hit = at + k * e, hit + e
        blk_of[o] = jnp.minimum(at, nblk - 1)
        hit_of[o] = hit.astype(F32)

    each(0, nz, block_for)

    locals_[1].wait()
    locals_[2].wait()

    def tile_of(j):
        c = pl.ds(pl.multiple_of(j * 128, 128), 128)
        gf = gv[:, c].astype(F32)
        h = gf * jax.nn.sigmoid(gf) * uv[:, c].astype(F32)
        hp[2 * j] = jnp.where(lane < 64, h[:fh], swap(h[fh:])).astype(BF16)
        hp[2 * j + 1] = jnp.where(lane < 64, swap(h[:fh]), h[fh:]).astype(BF16)

    both = min(known - 1, nblk // 2)

    def tile_and_token(j):
        tile_of(j)
        pass_tokens()

    each(0, both, tile_and_token)
    each(both, nblk // 2, tile_of)
    locals_[3].wait()

    def fill(o):
        at, hit = blk_of[o], hit_of[o]
        hs[o, :fh] = (hp[at].astype(F32) * hit).astype(BF16)
        x = (og3v[at].astype(F32) * hit).astype(BF16)
        for k in range(d_loc // 128):
            hs[o, fh + k * 64 : fh + (k + 1) * 64] = x[:, k * 128 : (k + 1) * 128]

    each(0, nz, fill)
    each(both, known - 1, lambda j: pass_tokens())
    for d in (0, 1):
        pl.semaphore_wait(tok.at[d], 1)

    def remote(src, dst, ssem, rsem, z, p):
        return pltpu.make_async_remote_copy(
            src_ref=src, dst_ref=dst, send_sem=ssem, recv_sem=rsem,
            device_id=(z, p), device_id_type=MESH,
        )

    far = wrap(g + nz // 2)

    def piece(ref, i):
        return ref.at[pl.ds(i * mid, mid)]

    def leg1(i):
        to = wrap(g + (quarter if i == 0 else -quarter))
        return remote(piece(hs.at[far], i), xb.at[i], xb_s.at[0, i], xb_r.at[0, i], to, m)

    def leg2(i):
        d = quarter if i == 0 else -quarter
        dst = piece(hr.at[wrap(g - d)], i)
        return remote(xb.at[i], dst, xb_s.at[1, i], xb_r.at[1, i], wrap(g + d), m)

    def leg2_in(i):
        ref = piece(hr.at[far], i)
        return remote(ref, ref, xb_s.at[1, i], xb_r.at[1, i], g, m)

    def block_copy(d):
        to = wrap(g + d)
        return remote(hs.at[to], hr.at[g], x_s.at[d], x_r.at[d], to, m)

    def block_in(d):
        ref = hr.at[wrap(g - d)]
        remote(ref, ref, x_s.at[d], x_r.at[d], g, m).wait_recv()

    def others(body):
        each(1, nz // 2, body)
        each(nz // 2 + 1, nz, body)

    for i in (0, 1):
        leg1(i).start()
    others(lambda d: block_copy(d).start())
    own_hs = local(hs.at[g], hr.at[g], 8)
    own_hs.start()

    def group_tables(j):
        hit, at = jnp.int32(0), jnp.int32(0)
        for k in range(nblk):
            s = soa[aob[j * nblk + k]]
            e = same(lax.div(s, own), g)
            hit, at = hit + e, at + e * lax.rem(s, own)
        slot_in[j] = jnp.minimum(at, own - 1)
        for l in range(own):
            mask_in[j * own + l] = (hit * same(at, l)).astype(F32)

    each(0, nz, group_tables)
    for k in range(nblk):
        o = owners[k]
        dist = lax.rem(sign * (g - o) + nz, nz)
        picked = jnp.minimum(jnp.maximum(dist - reach[0], 0), 1) * jnp.minimum(
            jnp.maximum(nz - reach[1] - dist, 0), 1
        )
        a_at[k] = picked * (g * own) + (1 - picked) * slots[k]
        sel_at[k] = picked * o + (1 - picked) * wrap(g - sign * (reach[0] + 1))
        sel_of[k] = picked.astype(F32)
        quad_of[k] = lax.div(o, 4)
        half_of[k] = lax.rem(lax.div(o, 2), 2).astype(F32)
        odd_of[k] = lax.rem(o, 2).astype(F32)

    cut = plane.size // 2
    each(1, cut, lambda s: plane.relay(s, 1))
    wring.relay(1)
    each(cut, plane.size - 1, lambda s: plane.relay(s, 1))
    plane.relay(plane.size - 1)
    plane.relay(plane.size)
    for c in locals_[4:]:
        c.wait()

    def grad_tile(j, k):
        return hr[j, fh + k * 64 : fh + (k + 1) * 64]

    def rows_of(ref, p):
        return ref.at[pl.ds(units * lax.div(p, 8), units), lax.rem(p, 8)]

    def part_copy(d):
        to = lax.rem(m + d, mp)
        return remote(rows_of(part, to), rsb.at[m], rs_s.at[d], rs_r.at[d], g, to)

    def part_in(d):
        ref = rsb.at[lax.rem(m + mp - d, mp)]
        remote(ref, ref, rs_s.at[d], rs_r.at[d], g, m).wait_recv()

    def fac_copy(d):
        to = lax.rem(m + d, mp)
        return remote(rows_of(fac, m), rows_of(fac, m), fg_s.at[d], fg_r.at[d], g, to)

    def fac_in(d):
        ref = rows_of(fac, lax.rem(m + mp - d, mp))
        remote(ref, ref, fg_s.at[d], fg_r.at[d], g, m).wait_recv()

    my_units = units * lax.div(m, 8)
    my_row = lax.rem(m, 8)

    def stage_partial():
        own_hs.wait()
        others(block_in)
        for i in (0, 1):
            leg2_in(i).wait_recv()

        def one(j):
            l = slot_in[j]
            z = dot(apk[l], hr[j, :fh], 0, 0)
            down = z[:64] + swap(z[64:])
            back = jnp.zeros((RANK, BLK), F32)
            for k in range(d_loc // 128):
                back += dot(bv[l, :, k * 128 : (k + 1) * 128], grad_tile(j, k), 1, 1)
            both = jnp.concatenate([down[:, :64], back], axis=1)
            part[j] = both.reshape(8, 8, 128)

        each(0, nz, one)
        each(1, mp, lambda d: part_copy(d).start())

    def stage_sum():
        rsb[m] = part[pl.ds(my_units, units), my_row]
        each(1, mp, part_in)
        total = lax.fori_loop(
            0, mp, lambda c, t: t + rsb[c], jnp.zeros((units, 8, 128), F32)
        )
        left = lax.broadcasted_iota(jnp.int32, (units, 8, 128), 2) < 64
        total = jnp.where(left, total, 2.0 * total).astype(BF16).astype(F32)
        fac[pl.ds(my_units, units), my_row] = total
        each(1, mp, lambda d: fac_copy(d).start())

    def back_copy(i):
        to = my_units + i
        return remote(fac.at[to, my_row], bk1.at[g], bk_s.at[i], bk_r.at[g], to, m)

    def back_in(o):
        remote(bk1.at[o], bk1.at[o], bk_s.at[0], bk_r.at[o], g, m).wait_recv()

    def stage_back():
        each(1, mp, fac_in)
        for i in range(units):
            @pl.when(my_units + i == g)
            def _():
                bk1[g] = fac[g, my_row]

            @pl.when(my_units + i != g)
            def _():
                back_copy(i).start()

    team = lax.div(g, units)

    def share_copy(d):
        to = lax.rem(m + d, mp)
        return remote(shs, bk2.at[:, my_row], bc_s.at[d], bc_r.at[my_row], g, to)

    def stage_share():
        @pl.when(lax.div(m, 8) == team)
        def _():
            each(1, nz, lambda d: back_in(wrap(g + d)))
            for i in range(nz // 4):
                pairs = [
                    jnp.where(lane64[:8] < 64, swap(bk1[4 * i + 2 * h]), bk1[4 * i + 2 * h + 1])
                    for h in (0, 1)
                ]
                x = jnp.concatenate(pairs, axis=0).astype(BF16)
                shs[i] = x
                bk2[i, my_row] = x
            each(1, mp, lambda d: share_copy(d).start())

    def stage_grads():
        gap[...] = jnp.zeros_like(gap)
        gb[...] = jnp.zeros_like(gb)

        def one(j):
            f = fac[j].reshape(RANK, 128)
            top = jnp.where(lane64 < 64, swap(f), 0.0).astype(BF16)
            bot = jnp.where(lane64 < 64, 0.0, f).astype(BF16)
            pa = dot(jnp.concatenate([top, bot], axis=0), hr[j, :fh], 1, 1)
            pa = pa.astype(BF16).astype(F32)
            down = f.astype(BF16)[:, :64]
            for k in range(d_loc // 128):
                c = slice(k * 128, (k + 1) * 128)
                pb = (2.0 * dot(down, grad_tile(j, k), 1, 0)).astype(BF16).astype(F32)
                for l in range(own):
                    gb[l, :, c] += pb * mask_in[j * own + l]
            for l in range(own):
                gap[l] += pa * mask_in[j * own + l]

        each(0, nz, one)
        for l in range(own):
            ga[l] = jnp.concatenate([gap[l, :64], gap[l, 64:]], axis=1)
        local(ga, ga_out, 9).start()
        local(gb, gb_out, 10).start()

    def picks():
        return ((0, wrap(g - sign * reach[0]), sign), (1, wrap(g + sign * reach[1]), -sign))

    def pick_copy(d, o, step, k):
        to = wrap(g + step * k)
        return remote(
            asend.at[d * 3 + k - 1], asel.at[o], sl_s.at[d, k - 1], sl_r.at[d, k - 1], to, m
        )

    def pick_send():
        for d, o, step in picks():
            for k in range(1, tail + 1):
                to = wrap(g + step * k)
                at = jnp.int32(0)
                for i in range(nblk):
                    s = soa[aob[to * nblk + i]]
                    at = at + same(lax.div(s, own), o) * lax.rem(s, own)
                asend[d * 3 + k - 1] = ab[o * own + jnp.minimum(at, own - 1)]
        for d, o, step in picks():
            for k in range(1, tail + 1):
                pick_copy(d, o, step, k).start()

    def pick_in():
        for k in range(1, tail + 1):
            for d, o in ((0, wrap(g - sign * (reach[0] + k))), (1, wrap(g + sign * (reach[1] + k)))):
                ref = asel.at[o]
                remote(ref, ref, sl_s.at[d, k - 1], sl_r.at[d, k - 1], g, m).wait_recv()

    def stage_side():
        pick_in()

        def row_in(t):
            ref = bk2.at[:, t]

            @pl.when(units_first + t != m)
            def _():
                remote(ref, ref, bc_s.at[0], bc_r.at[t], g, m).wait_recv()

        units_first = 8 * team

        each(0, 8, row_in)

        def first_of(k):
            near, sel = ab[a_at[k]].astype(F32), asel[sel_at[k]].astype(F32)
            return near * (1.0 - sel_of[k]) + sel * sel_of[k]

        def back_of(k, side):
            x = bk2[quad_of[k]].astype(F32)
            x = x[:, :8] * (1.0 - half_of[k]) + x[:, 8:] * half_of[k]
            x = x.reshape(RANK, 128)
            keep = odd_of[k] if side else 1.0 - odd_of[k]
            return x * keep + swap(x) * (1.0 - keep)

        def one(j):
            a1, a2 = first_of(2 * j), first_of(2 * j + 1)
            top = jnp.where(lane < 64, a1, swap(a2)).astype(BF16)
            bot = jnp.where(lane < 64, swap(a1), a2).astype(BF16)
            r = jnp.concatenate(
                [
                    jnp.where(lane64 < 64, back_of(2 * j, 0), 0.0),
                    jnp.where(lane64 < 64, 0.0, back_of(2 * j + 1, 1)),
                ],
                axis=0,
            ).astype(BF16)
            c = pl.ds(pl.multiple_of(j * 128, 128), 128)
            out[:fh, c] += dot(top, r, 1, 0)
            out[fh:, c] += dot(bot, r, 1, 0)

        each(0, nblk // 2, one)

    tile = 256 if rows % 256 == 0 else 128

    def multiply(z, h, fresh=False):
        x = wb[z, h]
        for t in range(rows // tile):
            c = slice(t * tile, (t + 1) * tile)
            y = dot(x, ogb[2 * z + h, c, :], 1, 1)
            if fresh:
                out[:, c] = y
            else:
                out[:, c] += y

    def multiply_step(s):
        def one(c):
            d, h = lax.div(c, 2), lax.rem(c, 2)
            multiply(wrap(g + (2 * d - 1) * s), h)

        each(0, 4, one)

    def stage_legs():
        for i in (0, 1):
            remote(xb.at[i], xb.at[i], xb_s.at[0, i], xb_r.at[0, i], g, m).wait_recv()
            leg2(i).start()

    stages = [stage_legs, stage_partial, stage_sum, stage_back, stage_share, stage_grads, stage_side]
    a_steps = [functools.partial(aring.relay, s) for s in range(1, reach[0] + 1)] + [pick_send]
    for s in range(1, nz // 2):
        if a_steps:
            a_steps.pop(0)()
        if s > 1:
            wring.relay(s)
        if s == 1:
            multiply(g, 0, True)
            multiply(g, 1)
        multiply_step(s)
        if stages and (len(stages) > 1 or not a_steps):
            stages.pop(0)()
    for f in a_steps + stages:
        f()
    wring.relay(nz // 2)
    each(0, 2, lambda c: multiply(far, c))

    local(ga, ga_out, 9).wait()
    local(gb, gb_out, 10).wait()
    plane.sent()
    wring.sent()
    aring.sent()
    others(lambda d: block_copy(d).wait_send())
    for i in (0, 1):
        leg1(i).wait_send()
        leg2(i).wait_send()
    each(1, mp, lambda d: part_copy(d).wait_send())
    each(1, mp, lambda d: fac_copy(d).wait_send())
    for i in range(units):
        @pl.when(my_units + i != g)
        def _():
            back_copy(i).wait_send()

    @pl.when(lax.div(m, 8) == team)
    def _():
        each(1, mp, lambda d: share_copy(d).wait_send())

    for d, o, step in picks():
        for k in range(1, tail + 1):
            pick_copy(d, o, step, k).wait_send()


def shards(og, gate, up, w, a, b, aob, soa):
    nz, mp = lax.axis_size("dp"), lax.axis_size("mp")
    rows, d_loc = og.shape
    ff = gate.shape[1]
    own = a.shape[0]
    nblk = rows // BLK
    fh = ff // 2
    send = fh + d_loc // 2
    units = nz * 8 // mp
    gate, up = gate.T, up.T
    vm = pl.BlockSpec(memory_space=pltpu.VMEM)
    sm = pl.BlockSpec(memory_space=pltpu.SMEM)
    hbm = pl.BlockSpec(memory_space=pl.ANY)
    dma = pltpu.SemaphoreType.DMA
    d_hidden, ga, gb = pl.pallas_call(
        functools.partial(kernel, nz, mp),
        out_shape=(
            jax.ShapeDtypeStruct((ff, rows), F32),
            jax.ShapeDtypeStruct((own, RANK, ff), F32),
            jax.ShapeDtypeStruct((own, RANK, d_loc), F32),
        ),
        in_specs=[sm] * 2 + [hbm] * 7,
        out_specs=(vm, hbm, hbm),
        scratch_shapes=[
            pltpu.VMEM((mp, rows, d_loc), BF16),
            pltpu.VMEM((nz, 2, ff, d_loc), BF16),
            pltpu.VMEM((nz * own, fh, 128), BF16),
            pltpu.VMEM((nz, fh, 128), BF16),
            pltpu.VMEM((own, fh, 128), BF16),
            pltpu.VMEM((6, fh, 128), BF16),
            pltpu.VMEM((nblk, BLK, d_loc), BF16),
            pltpu.VMEM((ff, rows), BF16),
            pltpu.VMEM((ff, rows), BF16),
            pltpu.VMEM((own, RANK, ff), BF16),
            pltpu.VMEM((own, RANK, d_loc), BF16),
            pltpu.VMEM((nblk, fh, 128), BF16),
            pltpu.VMEM((nz, send, 128), BF16),
            pltpu.VMEM((nz, send, 128), BF16),
            pltpu.VMEM((2, send // 2, 128), BF16),
            pltpu.VMEM((nz, 8, 8, 128), F32),
            pltpu.VMEM((mp, units, 8, 128), F32),
            pltpu.VMEM((nz, 8, 8, 128), F32),
            pltpu.VMEM((nz, 8, 128), F32),
            pltpu.VMEM((nz // 4, 16, 128), BF16),
            pltpu.VMEM((nz // 4, 8, 16, 128), BF16),
            pltpu.VMEM((own, 2 * RANK, fh), F32),
            pltpu.VMEM((own, RANK, ff), F32),
            pltpu.VMEM((own, RANK, d_loc), F32),
            pltpu.SMEM((nz,), jnp.int32),
            pltpu.SMEM((nz,), F32),
            pltpu.SMEM((nz,), jnp.int32),
            pltpu.SMEM((nz * own,), F32),
            pltpu.SMEM((nblk,), jnp.int32),
            pltpu.SMEM((nblk,), jnp.int32),
            pltpu.SMEM((nblk,), F32),
            pltpu.SMEM((nblk,), jnp.int32),
            pltpu.SMEM((nblk,), F32),
            pltpu.SMEM((nblk,), F32),
            dma((2, 2, mp // 2)), dma((2, 2, mp // 2)),
            dma((2, 2, nz // 2)), dma((2, 2, nz // 2)),
            dma((2, 2, nz // 2)), dma((2, 2, nz // 2)),
            dma((nz,)), dma((nz,)),
            dma((mp,)), dma((mp,)),
            dma((mp,)), dma((mp,)),
            dma((units,)), dma((nz,)),
            dma((mp,)), dma((8,)),
            dma((2, 3)), dma((2, 3)),
            dma((2, 2)), dma((2, 2)),
            dma((11,)),
            pltpu.SemaphoreType.REGULAR((2,)),
        ],
        compiler_params=pltpu.CompilerParams(
            collective_id=0, has_side_effects=True, vmem_limit_bytes=67_000_000
        ),
    )(aob, soa, og, og.reshape(nblk, BLK, d_loc), gate, up, w, a, b)
    gf, uf = gate.astype(F32), up.astype(F32)
    s = jax.nn.sigmoid(gf)
    d_gate = (d_hidden * uf * s * (1.0 + gf * (1.0 - s))).astype(BF16)
    d_up = (d_hidden * (gf * s)).astype(BF16)
    return d_gate.T, d_up.T, ga, gb


def solution(mesh):
    in_specs = (
        P("dp", "mp"),
        P("dp", "mp"),
        P("dp", "mp"),
        P("mp", "dp"),
        P("dp", None, "mp"),
        P("dp", None, "mp"),
        P(),
        P(),
    )
    out_specs = (P("dp", "mp"), P("dp", "mp"), P("dp", None, "mp"), P("dp", None, "mp"))
    return jax.shard_map(shards, mesh=mesh, in_specs=in_specs, out_specs=out_specs, check_vma=False)
```
